32 devices in a mesh: groups: 2 (over x), ta: 4 (over y, core), xy: 4 (over z).
Axes of the slice: x: 2, y: 2, z: 4, core: 2. Of those that a mesh axis runs over, the one named last changes fastest.
Arguments:
- sources: bfloat16 [8, 4, 4, 8, 96, 256], P('groups', 'ta', 'xy'), parts along dimension 0, may hold values from -24 to 24
- coarse_links: bfloat16 [18, 4, 4, 4, 8, 96, 96], P('groups', None, 'ta', 'xy'), parts along dimension 0, may hold values from -0.119628906 to 0.119628906
Outputs:
- solution: float32 [8, 4, 4, 8, 96, 256], P('groups', 'ta', 'xy'), parts along dimension 0
The draws below stay inside these ranges and needn't reach their ends.
There are 2 independent parts, one for each index of `groups`. The reference program is written for one: setup_inputs(seed, part) draws one part's arguments, and reference() takes and returns one part's arrays. A program takes and returns all parts, laid end to end along the dimension named above; each array names one. Nothing has to cross between parts.
All inputs are finite; a program needn't handle non-finite values.
Results may differ from the reference program's by a relative error of at most 0.0019.
The reference program's roundings to bfloat16 on the way count: a program that leaves them out, or rounds other values in their place, can miss the bound.
Values may be sent and summed in bfloat16 or wider, within the bound.
A program may use at most 128 MiB of HBM per device.

```python
import jax
import jax.numpy as jnp
from jax import lax

COMP = 96
RHS = 256
NY = 4
NZ = 8
DIRS = 9
ITERS = 2
NT = 4
NX = 4


def draw_sources(key, part):
    full_shape = (NY, NT, NX, NZ, COMP, RHS)
    subkeys = jax.random.split(jax.random.fold_in(key, 17), 4)
    rising = 1.5 * 3.0 ** (jnp.arange(NT, dtype=jnp.float32) / max(NT - 1, 1))
    rising = rising.reshape(1, NT, 1, 1, 1, 1)
    values = jax.random.normal(subkeys[3], full_shape, jnp.float32) * rising
    return jnp.clip(values, -24.0, 24.0).astype(jnp.bfloat16)


def shard_levels(rng, dims, cuts, smallest, high):
    def one(dim, blocks):
        heights = jax.random.uniform(jax.random.fold_in(jax.random.fold_in(rng, 6), dim), (blocks,), jnp.float32, smallest / len(cuts), high / len(cuts))
        return jnp.repeat(jnp.exp(heights), dims[dim] // blocks).reshape((-1,) + (1,) * (len(dims) - dim - 1))

    loudness = one(*cuts[0])
    for cut in cuts[1:]:
        loudness = loudness * one(*cut)
    return loudness


def noise(key, shape, width, bound, shards=(), kind=jnp.bfloat16):
    gain = shard_levels(key, shape, shards, -0.22, 0.18) if shards else 1.0
    array = jax.random.normal(key, shape, jnp.float32) * width * gain
    return jnp.minimum(jnp.maximum(array, -bound), bound).astype(kind)


def setup_inputs(seed: int = 0, part: int = 0) -> dict:
    splits = jax.random.split(jax.random.key(seed), 3)
    own_keys = jax.random.split(jax.random.fold_in(splits[2], part), 3)
    return {
        "sources": draw_sources(jax.random.fold_in(jax.random.fold_in(splits[2], part), 71), part),
        "coarse_links": noise(own_keys[1], (DIRS, NY, NT, NX, NZ, COMP, COMP), 0.02, 0.119628906, ((2, 4), (3, 4))),
    }


mass_term = 2.0
direction_moves = ((1, 1), (1, -1), (2, 1), (2, -1), (0, 1), (0, -1), (3, 1), (3, -1))

def link_product(link_field, vector, flipped):
    einsum_form = 'abcio,abcir->abcor' if flipped else 'abcoi,abcir->abcor'

    def one_plane(plane_pair):
        link_plane, values = plane_pair
        matrix = link_plane.astype(jnp.float32)
        entries = values.astype(jnp.float32)
        return jnp.einsum(einsum_form, matrix, entries, precision=lax.Precision.HIGHEST)
    return lax.map(one_plane, (link_field, vector))

def apply_forward(rounded, coarse_links):
    summed = mass_term * rounded.astype(jnp.float32) + link_product(coarse_links[0], rounded, False)
    for number in range(8):
        axis_number, sign_value = direction_moves[number]
        summed = summed + link_product(coarse_links[number + 1], jnp.roll(rounded, -sign_value, axis_number), False)
    return summed

def apply_adjoint(image_vec, coarse_links):
    summed = mass_term * image_vec.astype(jnp.float32) + link_product(coarse_links[0], image_vec, True)
    for number in range(8):
        axis_number, sign_value = direction_moves[number]
        adjoint_term = link_product(coarse_links[number + 1], image_vec, True).astype(jnp.bfloat16)
        summed = summed + jnp.roll(adjoint_term, sign_value, axis_number).astype(jnp.float32)
    return summed

def gram(left_vec, right_vec):
    left_rows = left_vec.reshape(-1, COMP, RHS)
    right_rows = right_vec.reshape(-1, COMP, RHS)
    return jnp.einsum('sir,sit->rt', left_rows, right_rows, precision=lax.Precision.HIGHEST)

def combine(vector, coefficients):
    return jnp.einsum('abcdir,rt->abcdit', vector, coefficients, precision=lax.Precision.HIGHEST)

def solve_spd(matrix, right_side):
    factor = jnp.linalg.cholesky(matrix)
    return jax.scipy.linalg.cho_solve((factor, True), right_side)

def reference(sources, coarse_links):
    residual = sources.astype(jnp.float32)
    solution = jnp.zeros_like(residual)
    search = residual
    energy = gram(residual, residual)
    for iteration in range(ITERS):
        rounded = search.astype(jnp.bfloat16)
        image_vec = apply_forward(rounded, coarse_links).astype(jnp.bfloat16)
        normal_image = apply_adjoint(image_vec, coarse_links)
        alpha_step = solve_spd(gram(search, normal_image), energy)
        solution = solution + combine(search, alpha_step)
        if iteration + 1 < ITERS:
            residual = residual - combine(normal_image, alpha_step)
            fresh_energy = gram(residual, residual)
            beta_step = solve_spd(energy, fresh_energy)
            search = residual + combine(search, beta_step)
            energy = fresh_energy
    return solution
```

```python
import functools

import jax
import jax.numpy as jnp
from jax import lax
from jax.experimental import pallas as pl
from jax.experimental.pallas import tpu as pltpu
from jax.sharding import PartitionSpec as P

mass_term = 2.0
MESH = pl.DeviceIdType.MESH
HI = lax.Precision.HIGHEST
f32 = jnp.float32
bf16 = jnp.bfloat16

HOPS = (("ta", 1), ("ta", -1), ("xy", 1), ("xy", -1))
CHUNKS = 8
EARLY = (2, 2, 3)
SUMS = 4

mul = functools.partial(lax.dot_general, preferred_element_type=f32)
STRAIGHT = (((1,), (0,)), ((), ()))
TURNED = (((0,), (0,)), ((), ()))


def iotas(n):
    return lax.broadcasted_iota(jnp.int32, (n, n), 0), lax.broadcasted_iota(jnp.int32, (n, n), 1)


def piece_rows(rhs, n_ta):
    return -(-(rhs // 2 + 8) // (8 * n_ta)) * 8


def krylov_kernel(sizes, ny, nz, src, links, first_ref, high_ref, low_ref, curvature_ref, fresh_ref,
                  r, lk, halo1, halo3, u_out, u_in, image, rounded, acc, full, normal, residual, gram_ref, cross_ref, work, inverse0,
                  sums, coef, packed, parts, total, planes, whole, local_sem, bulk_send, bulk_recv, sum_send, sum_recv):
    n_ta, n_xy = sizes["ta"], sizes["xy"]
    me = {axis: lax.axis_index(axis) for axis in sizes}
    n, comp, rhs = r.shape
    per = n // CHUNKS
    half = rhs // 2
    rows = piece_rows(rhs, n_ta)

    def peer(axis, off):
        return lax.rem(me[axis] + off + sizes[axis], sizes[axis])

    def sites(c):
        return pl.ds(c * per, per)

    def vector_copy(stage, d, c, source, halo):
        axis, step = HOPS[d]
        return pltpu.make_async_remote_copy(
            src_ref=source.at[sites(c)], dst_ref=halo.at[d, sites(c)],
            send_sem=bulk_send.at[stage, d, c], recv_sem=bulk_recv.at[stage, d, c],
            device_id={axis: peer(axis, -step)}, device_id_type=MESH)

    def product_copy(d, c):
        axis, step = HOPS[d]
        return pltpu.make_async_remote_copy(
            src_ref=u_out.at[d, sites(c)], dst_ref=u_in.at[d, sites(c)],
            send_sem=bulk_send.at[1, d, c], recv_sem=bulk_recv.at[1, d, c],
            device_id={axis: peer(axis, step)}, device_id_type=MESH)

    def copies(stage, c):
        if stage == 0:
            return [vector_copy(0, d, c, src, halo1) for d in (3, 2, 1, 0)]
        if stage == 1:
            return [product_copy(d, c) for d in (3, 2, 1, 0)]
        return [vector_copy(2, d, c, rounded, halo3) for d in (3, 2, 1, 0)]

    def send(stage, c):
        for copy in copies(stage, c):
            copy.start()

    def send_range(stage, lo, hi):
        @pl.loop(lo, hi)
        def _(c):
            send(stage, c)

    def arrive(stage, c):
        for copy in copies(stage, c):
            copy.wait_recv()

    def scatter(k, off):
        to = peer("ta", off)
        return pltpu.make_async_remote_copy(
            src_ref=packed.at[k, to], dst_ref=parts.at[k, off], send_sem=sum_send.at[k, 0, off],
            recv_sem=sum_recv.at[k, 0, off], device_id={"ta": to}, device_id_type=MESH)

    def spread(k, off):
        return pltpu.make_async_remote_copy(
            src_ref=total.at[k], dst_ref=planes.at[k, me["xy"]], send_sem=sum_send.at[k, 1, off],
            recv_sem=sum_recv.at[k, 1, off], device_id={"xy": peer("xy", off)}, device_id_type=MESH)

    def gather(k, off):
        return pltpu.make_async_remote_copy(
            src_ref=whole.at[k, me["ta"]], dst_ref=whole.at[k, me["ta"]], send_sem=sum_send.at[k, 2, off],
            recv_sem=sum_recv.at[k, 2, off], device_id={"ta": peer("ta", off)}, device_id_type=MESH)

    def came(make, k, off, ref):
        return pltpu.make_async_remote_copy(
            src_ref=ref, dst_ref=ref, send_sem=sum_send.at[k, make, off], recv_sem=sum_recv.at[k, make, off],
            device_id={"ta": peer("ta", 1)}, device_id_type=MESH)

    def sum_start(k, matrix):
        row, col = iotas(half)
        last = matrix[half:, half:]
        mixed = jnp.where(row >= col, matrix[:half, :half], last)
        diag = jnp.sum(jnp.where(row == col, last, 0.0), axis=0, keepdims=True)
        tail = jnp.concatenate([diag, jnp.zeros((1, half), f32)], axis=1)
        tail = jnp.broadcast_to(tail, (n_ta * rows - half, rhs))
        flat = jnp.concatenate([jnp.concatenate([mixed, matrix[half:, :half]], axis=1), tail], axis=0)
        for i in range(n_ta):
            packed[k, i] = flat[i * rows:(i + 1) * rows]
        for off in range(1, n_ta):
            scatter(k, off).start()

    def sum_spread(k):
        value = packed[k, me["ta"]]
        for off in range(1, n_ta):
            came(0, k, off, parts.at[k, off]).wait_recv()
            value = value + parts[k, off]
        total[k] = value
        for off in range(1, n_xy):
            spread(k, off).start()

    def sum_gather(k):
        for off in range(1, n_xy):
            came(1, k, off, planes.at[k, peer("xy", -off)]).wait_recv()
        planes[k, me["xy"]] = total[k]
        value = planes[k, 0]
        for i in range(1, n_xy):
            value = value + planes[k, i]
        whole[k, me["ta"]] = value
        for off in range(1, n_ta):
            gather(k, off).start()

    def sum_done(k):
        for off in range(1, n_ta):
            came(2, k, off, whole.at[k, peer("ta", -off)]).wait_recv()
        flat = jnp.concatenate([whole[k, i] for i in range(n_ta)], axis=0)
        row, col = iotas(half)
        mixed = flat[:half, :half]
        turned = mixed.T
        low = flat[:half, half:]
        first = jnp.where(row >= col, mixed, turned)
        last = jnp.where(row < col, mixed, turned)
        last = jnp.where(row == col, flat[half:half + 1, :half], last)
        return jnp.concatenate([jnp.concatenate([first, low.T], axis=1),
                                jnp.concatenate([low, last], axis=1)], axis=0)

    def sum_waits(k):
        for off in range(1, n_ta):
            scatter(k, off).wait_send()
            gather(k, off).wait_send()
        for off in range(1, n_xy):
            spread(k, off).wait_send()

    def gram(a, b):
        a, b = (v.reshape(-1, rhs) for v in (a, b))
        return mul(a, b, TURNED)

    def near(s):
        y, z = s // nz, lax.rem(s, nz)
        at = lambda i, j: lax.rem(i + ny, ny) * nz + lax.rem(j + nz, nz)
        return at(y + 1, z), at(y - 1, z), at(y, z + 1), at(y, z - 1)

    def apply_near(vector, value, lo, hi):
        @pl.loop(lo, hi)
        def _(s):
            total = mass_term * value(s) + mul(lk[0, s], vector[s], STRAIGHT)
            for k, other in enumerate(near(s)):
                total = total + mul(lk[k + 5, s], vector[other], STRAIGHT)
            acc[s] = total

    def apply_far(s, halo):
        total = acc[s]
        for d in range(4):
            total = total + mul(lk[d + 1, s], halo[d, s], STRAIGHT)
        return total

    def adjoint_near(lo, hi):
        @pl.loop(lo, hi)
        def _(s):
            here = image[s]
            total = mass_term * here.astype(f32) + mul(lk[0, s], here, TURNED)
            plus_y, minus_y, plus_z, minus_z = near(s)
            for k, origin in enumerate((minus_y, plus_y, minus_z, plus_z)):
                total = total + mul(lk[k + 5, origin], image[origin], TURNED).astype(bf16).astype(f32)
            acc[s] = total

    loads = [pltpu.make_async_copy(src, r, local_sem.at[0]), pltpu.make_async_copy(links, lk, local_sem.at[1])]
    for copy in loads:
        copy.start()
    barrier = pltpu.get_barrier_semaphore()
    for axis in ("ta", "xy"):
        for off in range(1, sizes[axis]):
            pl.semaphore_signal(barrier, inc=1, device_id={axis: peer(axis, off)}, device_id_type=MESH)
    pl.semaphore_wait(barrier, n_ta + n_xy - 2)

    def gram_add(high, low):
        gram_ref[...] += gram(high, high)
        cross_ref[...] += gram(low, high)

    def gram_clear():
        gram_ref[...] = jnp.zeros((rhs, rhs), f32)
        cross_ref[...] = jnp.zeros((rhs, rhs), f32)

    def times(high, low, k):
        high, low = high.reshape(-1, rhs), low.reshape(-1, rhs)
        out = mul(high, coef[2 * k], STRAIGHT) + mul(high, coef[2 * k + 1], STRAIGHT) + mul(low, coef[2 * k], STRAIGHT)
        return out.reshape(per, comp, rhs)

    def source_times(c, k):
        high = r[sites(c)].reshape(-1, rhs)
        return (mul(high, coef[2 * k], STRAIGHT) + mul(high, coef[2 * k + 1], STRAIGHT)).reshape(per, comp, rhs)

    def keep(k, value):
        high, low = split(value)
        coef[2 * k] = high
        coef[2 * k + 1] = low

    send_range(0, 0, EARLY[0])
    loads[0].wait()
    sum_start(0, gram(r[...], r[...]))
    loads[1].wait()
    apply_near(r, lambda s: r[s].astype(f32), 0, per * 2)
    sum_spread(0)
    send_range(0, EARLY[0], CHUNKS)
    apply_near(r, lambda s: r[s].astype(f32), per * 2, n)
    gram_clear()
    sum_gather(0)
    sums[0] = sum_done(0)
    eliminated(sums[0], work)
    inverse0[...] = work[0]

    def first(c):
        arrive(0, c)

        @pl.loop(0, per)
        def _(j):
            s = c * per + j
            value = apply_far(s, halo1)
            here, low = split(value)
            full[s] = value
            image[s] = here
            rounded[s] = low
            for d in range(4):
                u_out[d, s] = mul(lk[d + 1, s], here, TURNED).astype(bf16)

        gram_add(image[sites(c)], rounded[sites(c)])

    @pl.loop(0, EARLY[1])
    def _(c):
        first(c)
        send(1, c)

    @pl.loop(EARLY[1], CHUNKS)
    def _(c):
        first(c)

    sum_start(1, gram_ref[...] + 0.5 * (cross_ref[...] + cross_ref[...].T))
    adjoint_near(0, per * 2)
    sum_spread(1)
    send_range(1, EARLY[1], CHUNKS)
    adjoint_near(per * 2, n)
    gram_clear()

    def second(c):
        arrive(1, c)

        @pl.loop(0, per)
        def _(j):
            s = c * per + j
            value = acc[s]
            for d in range(4):
                value = value + u_in[d, s].astype(f32)
            normal[s] = value
            rounded[s] = value.astype(bf16)

    @pl.loop(0, EARLY[2])
    def _(c):
        second(c)
        send(2, c)

    sum_gather(1)
    sums[1] = sum_done(1)
    eliminated(sums[1], work)
    keep(0, solved(sums[1], work[0], sums[0]))

    @pl.loop(EARLY[2], CHUNKS)
    def _(c):
        second(c)

    @pl.loop(0, CHUNKS)
    def _(c):
        value, high = normal[sites(c)], rounded[sites(c)]
        here = r[sites(c)].astype(f32) - times(high, (value - high.astype(f32)).astype(bf16), 0)
        residual[sites(c)] = here
        gram_add(*split(here))

    sum_start(2, gram_ref[...] + cross_ref[...] + cross_ref[...].T)
    apply_near(rounded, lambda s: normal[s], 0, per * 2)
    sum_spread(2)
    send_range(2, EARLY[2], CHUNKS)
    apply_near(rounded, lambda s: normal[s], per * 2, n)
    gram_clear()
    for c in range(CHUNKS):
        for copy in copies(1, c):
            copy.wait_send()
    sum_gather(2)
    fresh_ref[...] = sum_done(2)
    beta = solved(sums[0], inverse0[...], fresh_ref[...])
    keep(1, beta)
    curvature_ref[...] = dot_t(beta, dot(sums[1], beta))

    @pl.loop(0, CHUNKS)
    def _(c):
        normal[sites(c)] = source_times(c, 0)
        high, low = split(residual[sites(c)] + source_times(c, 1))
        u_out[0, sites(c)] = high
        u_out[1, sites(c)] = low

    outs = [pltpu.make_async_copy(source, target, local_sem.at[2 + k]) for k, (source, target) in enumerate(
        ((normal, first_ref), (u_out.at[0], high_ref), (u_out.at[1], low_ref)))]
    for copy in outs:
        copy.start()

    @pl.loop(0, CHUNKS)
    def _(c):
        arrive(2, c)

        @pl.loop(0, per)
        def _(j):
            s = c * per + j
            acc[s] = apply_far(s, halo3)

        here = (full[sites(c)] - times(*split(acc[sites(c)]), 0)).astype(bf16)
        gram_ref[...] += gram(here, here)

    sum_start(3, gram_ref[...])
    sum_spread(3)
    sum_gather(3)
    for copy in outs:
        copy.wait()
    for stage in (0, 2):
        @pl.loop(0, CHUNKS)
        def _(c):
            for copy in copies(stage, c):
                copy.wait_send()
    curvature = sum_done(3) - curvature_ref[...]
    curvature_ref[...] = 0.5 * (curvature + curvature.T)
    for k in range(SUMS):
        sum_waits(k)


def krylov(sources, links, sizes):
    ny, nt, nx, nz, comp, rhs = sources.shape
    assert nt == 1 and nx == 1
    n = ny * nz
    n_ta, n_xy = sizes["ta"], sizes["xy"]
    rows = piece_rows(rhs, n_ta)
    anywhere = pl.BlockSpec(memory_space=pl.ANY)
    vmem = pl.BlockSpec(memory_space=pltpu.VMEM)
    slab = lambda *lead: pltpu.VMEM(lead + (n, comp, rhs), bf16)
    wide = pltpu.VMEM((n, comp, rhs), f32)
    pieces = lambda count: pltpu.VMEM((SUMS, count, rows, rhs), f32)
    most = max(n_ta, n_xy)
    square = lambda *lead: pltpu.VMEM(lead + (rhs, rhs), f32)
    return pl.pallas_call(
        functools.partial(krylov_kernel, sizes, ny, nz),
        out_shape=[jax.ShapeDtypeStruct((n, comp, rhs), d) for d in (f32, bf16, bf16)]
        + [jax.ShapeDtypeStruct((rhs, rhs), f32)] * 2,
        in_specs=[anywhere, anywhere],
        out_specs=[anywhere] * 3 + [vmem] * 2,
        scratch_shapes=[
            slab(), pltpu.VMEM((links.shape[0], n, comp, comp), bf16), slab(4), slab(4), slab(4), slab(4), slab(), slab(),
            wide, wide, wide, wide, square(), square(), square(2), square(), square(2), pltpu.VMEM((4, rhs, rhs), bf16),
            pieces(n_ta), pieces(n_ta), pltpu.VMEM((SUMS, rows, rhs), f32), pieces(n_xy), pieces(n_ta),
            pltpu.SemaphoreType.DMA((5,)), pltpu.SemaphoreType.DMA((3, 4, CHUNKS)), pltpu.SemaphoreType.DMA((3, 4, CHUNKS)),
            pltpu.SemaphoreType.DMA((SUMS, 3, most)), pltpu.SemaphoreType.DMA((SUMS, 3, most)),
        ],
        cost_estimate=pl.CostEstimate(flops=int(6e9), bytes_accessed=64 << 20, transcendentals=0),
        compiler_params=pltpu.CompilerParams(collective_id=0, has_side_effects=True, vmem_limit_bytes=67043328),
    )(sources.reshape(n, comp, rhs), links.reshape(links.shape[0], n, comp, comp))


dot = functools.partial(jnp.dot, precision=HI, preferred_element_type=f32)


def dot_t(a, b):
    return lax.dot_general(a, b, TURNED, precision=HI, preferred_element_type=f32)


def split(value):
    high = value.astype(bf16)
    return high, (value - high.astype(f32)).astype(bf16)


def scaled(a):
    row, col = iotas(a.shape[0])
    eye = jnp.where(row == col, 1.0, 0.0).astype(f32)
    diag = a * eye
    down = lax.rsqrt(jnp.sum(diag, axis=1, keepdims=True))
    across = lax.rsqrt(jnp.sum(diag, axis=0, keepdims=True))
    return a * down * across, eye, down, across


def eliminate(x_ref, n):
    row, col = iotas(n)

    def step(k, carry):
        m = x_ref[...]
        pivot_row = x_ref[pl.ds(k, 1), :]
        here = col == k
        pivot_col = jnp.sum(jnp.where(here, m, 0.0), axis=1, keepdims=True)
        hit = here[:1]
        inv = 1.0 / jnp.sum(jnp.where(hit, pivot_row, 0.0), axis=1, keepdims=True)
        line = jnp.where(hit, inv, pivot_row * inv)
        m = jnp.where(here, 0.0, m) - pivot_col * line
        x_ref[...] = jnp.where(row == k, line, m)
        return carry

    lax.fori_loop(0, n, step, 0)


def refined(a, x, eye, down, across):
    x = x + dot(x, eye - dot(a, x))
    return x * down * across


def eliminated(a, work):
    a, eye, down, across = scaled(a)
    work[0] = a
    work[1] = a
    eliminate(work.at[0], a.shape[0])
    work[0] = refined(work[1], work[0], eye, down, across)


def invert(a, x_ref, s_ref, p_ref):
    a, eye, down, across = scaled(a)
    s_ref[...] = a
    p_ref[...] = eye - a
    x_ref[...] = eye + p_ref[...]

    def square(_, carry):
        power = dot(p_ref[...], p_ref[...])
        p_ref[...] = power
        x_ref[...] = x_ref[...] + dot(x_ref[...], power)
        return carry

    lax.fori_loop(0, 3, square, 0)
    worst = jnp.max(jnp.abs(eye - dot(a, x_ref[...])))

    @pl.when(jnp.logical_not(worst < 1e-3))
    def _():
        x_ref[...] = s_ref[...]
        eliminate(x_ref, a.shape[0])

    return refined(s_ref[...], x_ref[...], eye, down, across)


def solved(a, inverse, right):
    out = dot(inverse, right)
    return out + dot(inverse, right - dot(a, out))


def closing_kernel(chunks, curvature_ref, fresh_ref, first_hbm, high_hbm, low_hbm, out_hbm,
                   first, high, low, coef, x_ref, s_ref, p_ref, load_sem, store_sem):
    n, comp, rhs = first.shape
    per = n // chunks
    loads = [pltpu.make_async_copy(source, target, load_sem.at[k]) for k, (source, target) in enumerate(
        ((first_hbm, first), (high_hbm, high), (low_hbm, low)))]
    for copy in loads:
        copy.start()
    curvature, fresh = curvature_ref[...], fresh_ref[...]
    alpha = solved(curvature, invert(curvature, x_ref, s_ref, p_ref), fresh)
    coef[0], coef[1] = split(alpha)
    for copy in loads:
        copy.wait()

    def store(c):
        return pltpu.make_async_copy(first.at[pl.ds(c * per, per)], out_hbm.at[pl.ds(c * per, per)], store_sem.at[c])

    @pl.loop(0, chunks)
    def _(c):
        here = pl.ds(c * per, per)
        left, rest = high[here].reshape(-1, rhs), low[here].reshape(-1, rhs)
        step = mul(left, coef[0], STRAIGHT) + mul(left, coef[1], STRAIGHT) + mul(rest, coef[0], STRAIGHT)
        first[here] = first[here] + step.reshape(per, comp, rhs)
        store(c).start()

    @pl.loop(0, chunks)
    def _(c):
        store(c).wait()


def closing(first, high, low, curvature, fresh):
    vmem, anywhere = pl.BlockSpec(memory_space=pltpu.VMEM), pl.BlockSpec(memory_space=pl.ANY)
    rhs = fresh.shape[0]
    return pl.pallas_call(
        functools.partial(closing_kernel, CHUNKS),
        out_shape=jax.ShapeDtypeStruct(first.shape, f32),
        in_specs=[vmem] * 2 + [anywhere] * 3,
        out_specs=anywhere,
        scratch_shapes=[pltpu.VMEM(first.shape, f32), pltpu.VMEM(first.shape, bf16), pltpu.VMEM(first.shape, bf16),
                        pltpu.VMEM((2, rhs, rhs), bf16)] + [pltpu.VMEM((rhs, rhs), f32)] * 3
        + [pltpu.SemaphoreType.DMA((3,)), pltpu.SemaphoreType.DMA((CHUNKS,))],
        cost_estimate=pl.CostEstimate(flops=int(4e9), bytes_accessed=10 << 20, transcendentals=0),
    )(curvature, fresh, first, high, low)


def solution(mesh):
    sizes = {axis: mesh.shape[axis] for axis in ("ta", "xy")}

    def body(sources, links):
        return closing(*krylov(sources, links, sizes)).reshape(sources.shape)

    return jax.shard_map(
        body,
        mesh=mesh,
        in_specs=(
            P("groups", "ta", "xy", None, None, None),
            P("groups", None, "ta", "xy", None, None, None),
        ),
        out_specs=P("groups", "ta", "xy", None, None, None),
        check_vma=False,
    )
```

```python
import functools

import jax
import jax.numpy as jnp
from jax import lax
from jax.experimental import pallas as pl
from jax.experimental.pallas import tpu as pltpu
from jax.sharding import PartitionSpec as P

mass_term = 2.0
MESH = pl.DeviceIdType.MESH
HI = lax.Precision.HIGHEST
f32 = jnp.float32
bf16 = jnp.bfloat16

HOPS = (("ta", 1), ("ta", -1), ("xy", 1), ("xy", -1))
CHUNKS = 8
EARLY = (2, 1, 2)
SUMS = 4

mul = functools.partial(lax.dot_general, preferred_element_type=f32)
STRAIGHT = (((1,), (0,)), ((), ()))
TURNED = (((0,), (0,)), ((), ()))


def iotas(n):
    return lax.broadcasted_iota(jnp.int32, (n, n), 0), lax.broadcasted_iota(jnp.int32, (n, n), 1)


def piece_rows(rhs, n_ta):
    return -(-(rhs + 1) // (8 * n_ta)) * 8


def krylov_kernel(sizes, ny, nz, src, links, first_ref, high_ref, low_ref, curvature_ref, fresh_ref,
                  r, lk, halo1, halo3, u_out, u_in, image, rounded, acc, full, normal, residual, gram_ref, cross_ref, work, inverse0,
                  sums, coef, packed, parts, total, planes, whole, local_sem, bulk_send, bulk_recv, sum_send, sum_recv):
    n_ta, n_xy = sizes["ta"], sizes["xy"]
    me = {axis: lax.axis_index(axis) for axis in sizes}
    n, comp, rhs = r.shape
    per = n // CHUNKS
    half = rhs // 2
    rows = piece_rows(rhs, n_ta)

    def peer(axis, off):
        return lax.rem(me[axis] + off + sizes[axis], sizes[axis])

    def sites(c):
        return pl.ds(c * per, per)

    def vector_copy(stage, d, c, source, halo):
        axis, step = HOPS[d]
        return pltpu.make_async_remote_copy(
            src_ref=source.at[sites(c)], dst_ref=halo.at[d, sites(c)],
            send_sem=bulk_send.at[stage, d, c], recv_sem=bulk_recv.at[stage, d, c],
            device_id={axis: peer(axis, -step)}, device_id_type=MESH)

    def product_copy(d, c):
        axis, step = HOPS[d]
        return pltpu.make_async_remote_copy(
            src_ref=u_out.at[d, sites(c)], dst_ref=u_in.at[d, sites(c)],
            send_sem=bulk_send.at[1, d, c], recv_sem=bulk_recv.at[1, d, c],
            device_id={axis: peer(axis, step)}, device_id_type=MESH)

    def copies(stage, c):
        if stage == 0:
            return [vector_copy(0, d, c, src, halo1) for d in (3, 2, 1, 0)]
        if stage == 1:
            return [product_copy(d, c) for d in (3, 2, 1, 0)]
        return [vector_copy(2, d, c, rounded, halo3) for d in (3, 2, 1, 0)]

    def send(stage, c):
        for copy in copies(stage, c):
            copy.start()

    def send_range(stage, lo, hi):
        @pl.loop(lo, hi)
        def _(c):
            send(stage, c)

    def arrive(stage, c):
        for copy in copies(stage, c):
            copy.wait_recv()

    def scatter(k, off):
        to = peer("ta", off)
        return pltpu.make_async_remote_copy(
            src_ref=packed.at[k, to], dst_ref=parts.at[k, off], send_sem=sum_send.at[k, 0, off],
            recv_sem=sum_recv.at[k, 0, off], device_id={"ta": to}, device_id_type=MESH)

    def spread(k, off):
        return pltpu.make_async_remote_copy(
            src_ref=total.at[k], dst_ref=planes.at[k, me["xy"]], send_sem=sum_send.at[k, 1, off],
            recv_sem=sum_recv.at[k, 1, off], device_id={"xy": peer("xy", off)}, device_id_type=MESH)

    def gather(k, off):
        return pltpu.make_async_remote_copy(
            src_ref=whole.at[k, me["ta"]], dst_ref=whole.at[k, me["ta"]], send_sem=sum_send.at[k, 2, off],
            recv_sem=sum_recv.at[k, 2, off], device_id={"ta": peer("ta", off)}, device_id_type=MESH)

    def came(make, k, off, ref):
        return pltpu.make_async_remote_copy(
            src_ref=ref, dst_ref=ref, send_sem=sum_send.at[k, make, off], recv_sem=sum_recv.at[k, make, off],
            device_id={"ta": peer("ta", 1)}, device_id_type=MESH)

    def sum_start(k, matrix):
        row, col = iotas(half)
        last = matrix[half:, half:]
        mixed = jnp.where(row >= col, matrix[:half, :half], last)
        diag = jnp.sum(jnp.where(row == col, last, 0.0), axis=0, keepdims=True)
        tail = jnp.broadcast_to(diag, (n_ta * rows - rhs, half))
        flat = jnp.concatenate([mixed, matrix[half:, :half], tail], axis=0)
        for i in range(n_ta):
            packed[k, i] = flat[i * rows:(i + 1) * rows]
        for off in range(1, n_ta):
            scatter(k, off).start()

    def sum_spread(k):
        value = packed[k, me["ta"]]
        for off in range(1, n_ta):
            came(0, k, off, parts.at[k, off]).wait_recv()
            value = value + parts[k, off]
        total[k] = value
        for off in range(1, n_xy):
            spread(k, off).start()

    def sum_gather(k):
        for off in range(1, n_xy):
            came(1, k, off, planes.at[k, peer("xy", -off)]).wait_recv()
        planes[k, me["xy"]] = total[k]
        value = planes[k, 0]
        for i in range(1, n_xy):
            value = value + planes[k, i]
        whole[k, me["ta"]] = value
        for off in range(1, n_ta):
            gather(k, off).start()

    def sum_done(k):
        for off in range(1, n_ta):
            came(2, k, off, whole.at[k, peer("ta", -off)]).wait_recv()
        flat = jnp.concatenate([whole[k, i] for i in range(n_ta)], axis=0)
        row, col = iotas(half)
        mixed, low = flat[:half], flat[half:rhs]
        turned = mixed.T
        first = jnp.where(row >= col, mixed, turned)
        last = jnp.where(row < col, mixed, turned)
        last = jnp.where(row == col, flat[rhs:rhs + 1], last)
        return jnp.concatenate([jnp.concatenate([first, low.T], axis=1),
                                jnp.concatenate([low, last], axis=1)], axis=0)

    def sum_waits(k):
        for off in range(1, n_ta):
            scatter(k, off).wait_send()
            gather(k, off).wait_send()
        for off in range(1, n_xy):
            spread(k, off).wait_send()

    def gram(a, b):
        a, b = (v.reshape(-1, rhs) for v in (a, b))
        return mul(a, b, TURNED)

    def near(s):
        y, z = s // nz, lax.rem(s, nz)
        at = lambda i, j: lax.rem(i + ny, ny) * nz + lax.rem(j + nz, nz)
        return at(y + 1, z), at(y - 1, z), at(y, z + 1), at(y, z - 1)

    def apply_near(vector, value, lo, hi):
        @pl.loop(lo, hi)
        def _(s):
            total = mass_term * value(s) + mul(lk[0, s], vector[s], STRAIGHT)
            for k, other in enumerate(near(s)):
                total = total + mul(lk[k + 5, s], vector[other], STRAIGHT)
            acc[s] = total

    def apply_far(s, halo):
        total = acc[s]
        for d in range(4):
            total = total + mul(lk[d + 1, s], halo[d, s], STRAIGHT)
        return total

    def adjoint_near(lo, hi):
        @pl.loop(lo, hi)
        def _(s):
            here = image[s]
            total = mass_term * here.astype(f32) + mul(lk[0, s], here, TURNED)
            plus_y, minus_y, plus_z, minus_z = near(s)
            for k, origin in enumerate((minus_y, plus_y, minus_z, plus_z)):
                total = total + mul(lk[k + 5, origin], image[origin], TURNED).astype(bf16).astype(f32)
            acc[s] = total

    loads = [pltpu.make_async_copy(src, r, local_sem.at[0]), pltpu.make_async_copy(links, lk, local_sem.at[1])]
    for copy in loads:
        copy.start()
    barrier = pltpu.get_barrier_semaphore()
    for axis in ("ta", "xy"):
        for off in range(1, sizes[axis]):
            pl.semaphore_signal(barrier, inc=1, device_id={axis: peer(axis, off)}, device_id_type=MESH)
    pl.semaphore_wait(barrier, n_ta + n_xy - 2)

    def gram_add(high, low):
        gram_ref[...] += gram(high, high)
        cross_ref[...] += gram(low, high)

    def gram_clear():
        gram_ref[...] = jnp.zeros((rhs, rhs), f32)
        cross_ref[...] = jnp.zeros((rhs, rhs), f32)

    def times(high, low, k):
        high, low = high.reshape(-1, rhs), low.reshape(-1, rhs)
        out = mul(high, coef[2 * k], STRAIGHT) + mul(high, coef[2 * k + 1], STRAIGHT) + mul(low, coef[2 * k], STRAIGHT)
        return out.reshape(per, comp, rhs)

    def source_times(c, k):
        high = r[sites(c)].reshape(-1, rhs)
        return (mul(high, coef[2 * k], STRAIGHT) + mul(high, coef[2 * k + 1], STRAIGHT)).reshape(per, comp, rhs)

    def keep(k, value):
        high, low = split(value)
        coef[2 * k] = high
        coef[2 * k + 1] = low

    def share(i, count, whole=rhs):
        return whole * i // count, whole * (i + 1) // count

    send_range(0, 0, EARLY[0])
    loads[0].wait()
    sum_start(0, gram(r[...], r[...]))
    loads[1].wait()
    apply_near(r, lambda s: r[s].astype(f32), 0, per * 2)
    sum_spread(0)
    send_range(0, EARLY[0], CHUNKS)
    apply_near(r, lambda s: r[s].astype(f32), per * 2, n)
    gram_clear()
    def first(c):
        arrive(0, c)

        @pl.loop(0, per)
        def _(j):
            s = c * per + j
            value = apply_far(s, halo1)
            here, low = split(value)
            full[s] = value
            image[s] = here
            rounded[s] = low
            for d in range(4):
                u_out[d, s] = mul(lk[d + 1, s], here, TURNED).astype(bf16)

        gram_add(image[sites(c)], rounded[sites(c)])

    for c in range(CHUNKS):
        first(c)
        if c < EARLY[1]:
            send(1, c)
        if c == EARLY[0] - 1:
            sum_gather(0)
        if c == EARLY[0]:
            sums[0] = sum_done(0)
            elimination_begin(sums[0], work)
        if EARLY[0] <= c < CHUNKS - 1:
            eliminate(work.at[0], *share(c - EARLY[0], CHUNKS - EARLY[0]))

    sum_start(1, gram_ref[...] + 0.5 * (cross_ref[...] + cross_ref[...].T))
    adjoint_near(0, per * 2)
    sum_spread(1)
    send_range(1, EARLY[1], CHUNKS)
    adjoint_near(per * 2, n)
    gram_clear()
    eliminate(work.at[0], share(CHUNKS - 1 - EARLY[0], CHUNKS - EARLY[0])[0], rhs)
    inverse0[...] = elimination_end(sums[0], work)

    def second(c):
        arrive(1, c)

        @pl.loop(0, per)
        def _(j):
            s = c * per + j
            value = acc[s]
            for d in range(4):
                value = value + u_in[d, s].astype(f32)
            normal[s] = value
            rounded[s] = value.astype(bf16)

    def third(c):
        value, high = normal[sites(c)], rounded[sites(c)]
        here = r[sites(c)].astype(f32) - times(high, (value - high.astype(f32)).astype(bf16), 0)
        residual[sites(c)] = here
        gram_add(*split(here))

    ahead = CHUNKS - 2
    for c in range(ahead):
        second(c)
        if c < EARLY[2]:
            send(2, c)
        if c == 0:
            sum_gather(1)
            sums[1] = sum_done(1)
            elimination_begin(sums[1], work)
        eliminate(work.at[0], *share(c, ahead))
    keep(0, solved(sums[1], elimination_end(sums[1], work), sums[0]))

    @pl.loop(0, ahead)
    def _(c):
        third(c)

    @pl.loop(ahead, CHUNKS)
    def _(c):
        second(c)
        third(c)

    sum_start(2, gram_ref[...] + cross_ref[...] + cross_ref[...].T)
    apply_near(rounded, lambda s: normal[s], 0, per * 2)
    sum_spread(2)
    send_range(2, EARLY[2], CHUNKS)
    apply_near(rounded, lambda s: normal[s], per * 2, n)
    gram_clear()
    @pl.loop(0, CHUNKS)
    def _(c):
        for copy in copies(1, c):
            copy.wait_send()

    def fourth(c):
        arrive(2, c)

        @pl.loop(0, per)
        def _(j):
            s = c * per + j
            acc[s] = apply_far(s, halo3)

        here = (full[sites(c)] - times(*split(acc[sites(c)]), 0)).astype(bf16)
        gram_ref[...] += gram(here, here)

    def fifth(c):
        normal[sites(c)] = source_times(c, 0)
        high, low = split(residual[sites(c)] + source_times(c, 1))
        u_out[0, sites(c)] = high
        u_out[1, sites(c)] = low

    outs = [pltpu.make_async_copy(source, target, local_sem.at[2 + k]) for k, (source, target) in enumerate(
        ((normal, first_ref), (u_out.at[0], high_ref), (u_out.at[1], low_ref)))]
    begin = EARLY[2] + 1
    for c in range(CHUNKS):
        fourth(c)
        if c == EARLY[2] - 1:
            sum_gather(2)
        if c == EARLY[2]:
            fresh_ref[...] = sum_done(2)
            beta = solved(sums[0], inverse0[...], fresh_ref[...])
            keep(1, beta)
            curvature_ref[...] = dot_t(beta, dot(sums[1], beta))
        if begin <= c < CHUNKS - 1:
            lo, hi = share(c - begin, CHUNKS - 1 - begin, CHUNKS)
            pl.loop(lo, hi)(fifth)
        if c == CHUNKS - 2:
            for copy in outs:
                copy.start()

    sum_start(3, gram_ref[...])
    sum_spread(3)
    sum_gather(3)
    for copy in outs:
        copy.wait()
    for stage in (0, 2):
        @pl.loop(0, CHUNKS)
        def _(c):
            for copy in copies(stage, c):
                copy.wait_send()
    curvature = sum_done(3) - curvature_ref[...]
    curvature_ref[...] = 0.5 * (curvature + curvature.T)
    for k in range(SUMS):
        sum_waits(k)


def krylov(sources, links, sizes):
    ny, nt, nx, nz, comp, rhs = sources.shape
    assert nt == 1 and nx == 1
    n = ny * nz
    n_ta, n_xy = sizes["ta"], sizes["xy"]
    rows = piece_rows(rhs, n_ta)
    anywhere = pl.BlockSpec(memory_space=pl.ANY)
    vmem = pl.BlockSpec(memory_space=pltpu.VMEM)
    slab = lambda *lead: pltpu.VMEM(lead + (n, comp, rhs), bf16)
    wide = pltpu.VMEM((n, comp, rhs), f32)
    pieces = lambda count: pltpu.VMEM((SUMS, count, rows, rhs // 2), f32)
    most = max(n_ta, n_xy)
    square = lambda *lead: pltpu.VMEM(lead + (rhs, rhs), f32)
    return pl.pallas_call(
        functools.partial(krylov_kernel, sizes, ny, nz),
        out_shape=[jax.ShapeDtypeStruct((n, comp, rhs), d) for d in (f32, bf16, bf16)]
        + [jax.ShapeDtypeStruct((rhs, rhs), f32)] * 2,
        in_specs=[anywhere, anywhere],
        out_specs=[anywhere] * 3 + [vmem] * 2,
        scratch_shapes=[
            slab(), pltpu.VMEM((links.shape[0], n, comp, comp), bf16), slab(4), slab(4), slab(4), slab(4), slab(), slab(),
            wide, wide, wide, wide, square(), square(), square(2), square(), square(2), pltpu.VMEM((4, rhs, rhs), bf16),
            pieces(n_ta), pieces(n_ta), pltpu.VMEM((SUMS, rows, rhs // 2), f32), pieces(n_xy), pieces(n_ta),
            pltpu.SemaphoreType.DMA((5,)), pltpu.SemaphoreType.DMA((3, 4, CHUNKS)), pltpu.SemaphoreType.DMA((3, 4, CHUNKS)),
            pltpu.SemaphoreType.DMA((SUMS, 3, most)), pltpu.SemaphoreType.DMA((SUMS, 3, most)),
        ],
        cost_estimate=pl.CostEstimate(flops=int(6e9), bytes_accessed=64 << 20, transcendentals=0),
        compiler_params=pltpu.CompilerParams(collective_id=0, has_side_effects=True, vmem_limit_bytes=67043328),
    )(sources.reshape(n, comp, rhs), links.reshape(links.shape[0], n, comp, comp))


dot = functools.partial(jnp.dot, precision=HI, preferred_element_type=f32)


def dot_t(a, b):
    return lax.dot_general(a, b, TURNED, precision=HI, preferred_element_type=f32)


def split(value):
    high = value.astype(bf16)
    return high, (value - high.astype(f32)).astype(bf16)


def scaled(a):
    row, col = iotas(a.shape[0])
    eye = jnp.where(row == col, 1.0, 0.0).astype(f32)
    diag = a * eye
    down = lax.rsqrt(jnp.sum(diag, axis=1, keepdims=True))
    across = lax.rsqrt(jnp.sum(diag, axis=0, keepdims=True))
    return a * down * across, eye, down, across


def eliminate(x_ref, lo, hi):
    row, col = iotas(x_ref.shape[0])

    def step(k, carry):
        m = x_ref[...]
        pivot_row = x_ref[pl.ds(k, 1), :]
        here = col == k
        pivot_col = jnp.sum(jnp.where(here, m, 0.0), axis=1, keepdims=True)
        hit = here[:1]
        inv = 1.0 / jnp.sum(jnp.where(hit, pivot_row, 0.0), axis=1, keepdims=True)
        line = jnp.where(hit, inv, pivot_row * inv)
        m = jnp.where(here, 0.0, m) - pivot_col * line
        x_ref[...] = jnp.where(row == k, line, m)
        return carry

    lax.fori_loop(lo, hi, step, 0)


def elimination_begin(a, work):
    work[0] = work[1] = scaled(a)[0]


def elimination_end(a, work):
    _, eye, down, across = scaled(a)
    return refined(work[1], work[0], eye, down, across)


def refined(a, x, eye, down, across):
    x = x + dot(x, eye - dot(a, x))
    return x * down * across


def solved(a, inverse, right):
    out = dot(inverse, right)
    return out + dot(inverse, right - dot(a, out))


def solve(a, right, x_ref, s_ref, out_ref):
    s, eye, down, across = scaled(a)
    power = eye - s
    near = power.astype(bf16)
    square = mul(near, near, STRAIGHT)
    near2 = square.astype(bf16)
    fourth = mul(near2, near2, STRAIGHT).astype(bf16)
    inverse = eye + power + square + mul(near, near2, STRAIGHT)
    inverse = (inverse + mul(inverse.astype(bf16), fourth, STRAIGHT)).astype(bf16)
    off = jnp.abs(eye - mul(s.astype(bf16), inverse, STRAIGHT))
    worst = jnp.max(jnp.sum(off, axis=1, keepdims=True))
    right = right * down
    x = mul(inverse, right.astype(bf16), STRAIGHT)
    for _ in range(2):
        x = x + mul(inverse, (right - dot(s, x)).astype(bf16), STRAIGHT)
    out_ref[...] = x * down

    @pl.when(jnp.logical_not(worst < 0.05))
    def _():
        s_ref[...] = s
        x_ref[...] = s
        eliminate(x_ref, 0, a.shape[0])
        x = refined(s_ref[...], x_ref[...], eye, 1.0, 1.0)
        out_ref[...] = solved(s_ref[...], x, right) * down


def closing_kernel(chunks, curvature_ref, fresh_ref, first_hbm, high_hbm, low_hbm, out_hbm,
                   first, high, low, coef, x_ref, s_ref, alpha_ref, load_sem, store_sem):
    n, comp, rhs = first.shape
    per = n // chunks
    loads = [pltpu.make_async_copy(source, target, load_sem.at[k]) for k, (source, target) in enumerate(
        ((first_hbm, first), (high_hbm, high), (low_hbm, low)))]
    for copy in loads:
        copy.start()
    solve(curvature_ref[...], fresh_ref[...], x_ref, s_ref, alpha_ref)
    coef[0], coef[1] = split(alpha_ref[...])
    for copy in loads:
        copy.wait()

    def store(c):
        return pltpu.make_async_copy(first.at[pl.ds(c * per, per)], out_hbm.at[pl.ds(c * per, per)], store_sem.at[c])

    @pl.loop(0, chunks)
    def _(c):
        here = pl.ds(c * per, per)
        left, rest = high[here].reshape(-1, rhs), low[here].reshape(-1, rhs)
        step = mul(left, coef[0], STRAIGHT) + mul(left, coef[1], STRAIGHT) + mul(rest, coef[0], STRAIGHT)
        first[here] = first[here] + step.reshape(per, comp, rhs)
        store(c).start()

    @pl.loop(0, chunks)
    def _(c):
        store(c).wait()


def closing(first, high, low, curvature, fresh):
    vmem, anywhere = pl.BlockSpec(memory_space=pltpu.VMEM), pl.BlockSpec(memory_space=pl.ANY)
    rhs = fresh.shape[0]
    return pl.pallas_call(
        functools.partial(closing_kernel, CHUNKS),
        out_shape=jax.ShapeDtypeStruct(first.shape, f32),
        in_specs=[vmem] * 2 + [anywhere] * 3,
        out_specs=anywhere,
        scratch_shapes=[pltpu.VMEM(first.shape, f32), pltpu.VMEM(first.shape, bf16), pltpu.VMEM(first.shape, bf16),
                        pltpu.VMEM((2, rhs, rhs), bf16)] + [pltpu.VMEM((rhs, rhs), f32)] * 3
        + [pltpu.SemaphoreType.DMA((3,)), pltpu.SemaphoreType.DMA((CHUNKS,))],
        cost_estimate=pl.CostEstimate(flops=int(4e9), bytes_accessed=10 << 20, transcendentals=0),
    )(curvature, fresh, first, high, low)


def solution(mesh):
    sizes = {axis: mesh.shape[axis] for axis in ("ta", "xy")}

    def body(sources, links):
        return closing(*krylov(sources, links, sizes)).reshape(sources.shape)

    return jax.shard_map(
        body,
        mesh=mesh,
        in_specs=(
            P("groups", "ta", "xy", None, None, None),
            P("groups", None, "ta", "xy", None, None, None),
        ),
        out_specs=P("groups", "ta", "xy", None, None, None),
        check_vma=False,
    )
```

```python
import functools

import jax
import jax.numpy as jnp
from jax import lax
from jax.experimental import pallas as pl
from jax.experimental.pallas import tpu as pltpu
from jax.sharding import PartitionSpec as P

mass_term = 2.0
MESH = pl.DeviceIdType.MESH
HI = lax.Precision.HIGHEST
f32 = jnp.float32
bf16 = jnp.bfloat16

HOPS = (("ta", 1), ("ta", -1), ("xy", 1), ("xy", -1))
CHUNKS = 8
EARLY = (2, 3, 4)
SUMS = 4

mul = functools.partial(lax.dot_general, preferred_element_type=f32)
STRAIGHT = (((1,), (0,)), ((), ()))
TURNED = (((0,), (0,)), ((), ()))


def iotas(n):
    return lax.broadcasted_iota(jnp.int32, (n, n), 0), lax.broadcasted_iota(jnp.int32, (n, n), 1)


def piece_rows(rhs, n_ta):
    return -(-(rhs + 1) // (8 * n_ta)) * 8


def krylov_kernel(sizes, ny, nz, src, links, first_ref, high_ref, low_ref, curvature_ref, fresh_ref,
                  r, lk, halo1, halo3, u_out, u_in, image, rounded, acc, full, normal, residual, gram_ref, cross_ref, work, inverse0,
                  sums, coef, packed, parts, total, planes, whole, local_sem, bulk_send, bulk_recv, sum_send, sum_recv):
    n_ta, n_xy = sizes["ta"], sizes["xy"]
    me = {axis: lax.axis_index(axis) for axis in sizes}
    n, comp, rhs = r.shape
    per = n // CHUNKS
    half = rhs // 2
    rows = piece_rows(rhs, n_ta)

    def peer(axis, off):
        return lax.rem(me[axis] + off + sizes[axis], sizes[axis])

    def sites(c):
        return pl.ds(c * per, per)

    def vector_copy(stage, d, c, source, halo):
        axis, step = HOPS[d]
        return pltpu.make_async_remote_copy(
            src_ref=source.at[sites(c)], dst_ref=halo.at[d, sites(c)],
            send_sem=bulk_send.at[stage, d, c], recv_sem=bulk_recv.at[stage, d, c],
            device_id={axis: peer(axis, -step)}, device_id_type=MESH)

    def product_copy(d, c):
        axis, step = HOPS[d]
        return pltpu.make_async_remote_copy(
            src_ref=u_out.at[d, sites(c)], dst_ref=u_in.at[d, sites(c)],
            send_sem=bulk_send.at[1, d, c], recv_sem=bulk_recv.at[1, d, c],
            device_id={axis: peer(axis, step)}, device_id_type=MESH)

    def copies(stage, c):
        if stage == 0:
            return [vector_copy(0, d, c, src, halo1) for d in (3, 2, 1, 0)]
        if stage == 1:
            return [product_copy(d, c) for d in (3, 2, 1, 0)]
        return [vector_copy(2, d, c, rounded, halo3) for d in (3, 2, 1, 0)]

    def send(stage, c):
        for copy in copies(stage, c):
            copy.start()

    def send_range(stage, lo, hi):
        @pl.loop(lo, hi)
        def _(c):
            send(stage, c)

    def arrive(stage, c):
        for copy in copies(stage, c):
            copy.wait_recv()

    def scatter(k, off):
        to = peer("ta", off)
        return pltpu.make_async_remote_copy(
            src_ref=packed.at[k, to], dst_ref=parts.at[k, off], send_sem=sum_send.at[k, 0, off],
            recv_sem=sum_recv.at[k, 0, off], device_id={"ta": to}, device_id_type=MESH)

    def spread(k, off):
        return pltpu.make_async_remote_copy(
            src_ref=total.at[k], dst_ref=planes.at[k, me["xy"]], send_sem=sum_send.at[k, 1, off],
            recv_sem=sum_recv.at[k, 1, off], device_id={"xy": peer("xy", off)}, device_id_type=MESH)

    def gather(k, off):
        return pltpu.make_async_remote_copy(
            src_ref=whole.at[k, me["ta"]], dst_ref=whole.at[k, me["ta"]], send_sem=sum_send.at[k, 2, off],
            recv_sem=sum_recv.at[k, 2, off], device_id={"ta": peer("ta", off)}, device_id_type=MESH)

    def came(make, k, off, ref):
        return pltpu.make_async_remote_copy(
            src_ref=ref, dst_ref=ref, send_sem=sum_send.at[k, make, off], recv_sem=sum_recv.at[k, make, off],
            device_id={"ta": peer("ta", 1)}, device_id_type=MESH)

    def sum_start(k, matrix):
        row, col = iotas(half)
        last = matrix[half:, half:]
        mixed = jnp.where(row >= col, matrix[:half, :half], last)
        diag = jnp.sum(jnp.where(row == col, last, 0.0), axis=0, keepdims=True)
        tail = jnp.broadcast_to(diag, (n_ta * rows - rhs, half))
        flat = jnp.concatenate([mixed, matrix[half:, :half], tail], axis=0)
        for i in range(n_ta):
            packed[k, i] = flat[i * rows:(i + 1) * rows]
        for off in range(1, n_ta):
            scatter(k, off).start()

    def sum_spread(k):
        value = packed[k, me["ta"]]
        for off in range(1, n_ta):
            came(0, k, off, parts.at[k, off]).wait_recv()
            value = value + parts[k, off]
        total[k] = value
        for off in range(1, n_xy):
            spread(k, off).start()

    def sum_gather(k):
        for off in range(1, n_xy):
            came(1, k, off, planes.at[k, peer("xy", -off)]).wait_recv()
        planes[k, me["xy"]] = total[k]
        value = planes[k, 0]
        for i in range(1, n_xy):
            value = value + planes[k, i]
        whole[k, me["ta"]] = value
        for off in range(1, n_ta):
            gather(k, off).start()

    def sum_done(k):
        for off in range(1, n_ta):
            came(2, k, off, whole.at[k, peer("ta", -off)]).wait_recv()
        flat = jnp.concatenate([whole[k, i] for i in range(n_ta)], axis=0)
        row, col = iotas(half)
        mixed, low = flat[:half], flat[half:rhs]
        turned = mixed.T
        first = jnp.where(row >= col, mixed, turned)
        last = jnp.where(row < col, mixed, turned)
        last = jnp.where(row == col, flat[rhs:rhs + 1], last)
        return jnp.concatenate([jnp.concatenate([first, low.T], axis=1),
                                jnp.concatenate([low, last], axis=1)], axis=0)

    def sum_waits(k):
        for off in range(1, n_ta):
            scatter(k, off).wait_send()
            gather(k, off).wait_send()
        for off in range(1, n_xy):
            spread(k, off).wait_send()

    def gram(a, b):
        a, b = (v.reshape(-1, rhs) for v in (a, b))
        return mul(a, b, TURNED)

    def near(s):
        y, z = s // nz, lax.rem(s, nz)
        at = lambda i, j: lax.rem(i + ny, ny) * nz + lax.rem(j + nz, nz)
        return at(y + 1, z), at(y - 1, z), at(y, z + 1), at(y, z - 1)

    def apply_near(vector, value, lo, hi):
        @pl.loop(lo, hi)
        def _(s):
            total = mass_term * value(s) + mul(lk[0, s], vector[s], STRAIGHT)
            for k, other in enumerate(near(s)):
                total = total + mul(lk[k + 5, s], vector[other], STRAIGHT)
            acc[s] = total

    def apply_far(s, halo):
        total = acc[s]
        for d in range(4):
            total = total + mul(lk[d + 1, s], halo[d, s], STRAIGHT)
        return total

    def adjoint_near(lo, hi):
        @pl.loop(lo, hi)
        def _(s):
            here = image[s]
            total = mass_term * here.astype(f32) + mul(lk[0, s], here, TURNED)
            plus_y, minus_y, plus_z, minus_z = near(s)
            for k, origin in enumerate((minus_y, plus_y, minus_z, plus_z)):
                total = total + mul(lk[k + 5, origin], image[origin], TURNED).astype(bf16).astype(f32)
            acc[s] = total

    loads = [pltpu.make_async_copy(src, r, local_sem.at[0]), pltpu.make_async_copy(links, lk, local_sem.at[1])]
    for copy in loads:
        copy.start()
    barrier = pltpu.get_barrier_semaphore()
    for axis in ("ta", "xy"):
        for off in range(1, sizes[axis]):
            pl.semaphore_signal(barrier, inc=1, device_id={axis: peer(axis, off)}, device_id_type=MESH)
    pl.semaphore_wait(barrier, n_ta + n_xy - 2)

    def gram_add(high, low):
        gram_ref[...] += gram(high, high)
        cross_ref[...] += gram(low, high)

    def gram_clear():
        gram_ref[...] = jnp.zeros((rhs, rhs), f32)
        cross_ref[...] = jnp.zeros((rhs, rhs), f32)

    def times(high, low, k):
        high, low = high.reshape(-1, rhs), low.reshape(-1, rhs)
        out = mul(high, coef[2 * k], STRAIGHT) + mul(high, coef[2 * k + 1], STRAIGHT) + mul(low, coef[2 * k], STRAIGHT)
        return out.reshape(per, comp, rhs)

    def source_times(c, k):
        high = r[sites(c)].reshape(-1, rhs)
        return (mul(high, coef[2 * k], STRAIGHT) + mul(high, coef[2 * k + 1], STRAIGHT)).reshape(per, comp, rhs)

    def keep(k, value):
        high, low = split(value)
        coef[2 * k] = high
        coef[2 * k + 1] = low

    def share(i, count, whole=rhs):
        return whole * i // count, whole * (i + 1) // count

    send_range(0, 0, EARLY[0])
    loads[0].wait()
    sum_start(0, gram(r[...], r[...]))
    loads[1].wait()
    apply_near(r, lambda s: r[s].astype(f32), 0, per * 2)
    sum_spread(0)
    send_range(0, EARLY[0], CHUNKS)
    apply_near(r, lambda s: r[s].astype(f32), per * 2, n)
    gram_clear()
    def first(c):
        arrive(0, c)

        @pl.loop(0, per)
        def _(j):
            s = c * per + j
            value = apply_far(s, halo1)
            here, low = split(value)
            full[s] = value
            image[s] = here
            rounded[s] = low
            for d in range(4):
                u_out[d, s] = mul(lk[d + 1, s], here, TURNED).astype(bf16)

        gram_add(image[sites(c)], rounded[sites(c)])

    for c in range(CHUNKS):
        first(c)
        if c < EARLY[1]:
            send(1, c)
        if c == EARLY[0] - 1:
            sum_gather(0)
        if c == EARLY[0]:
            sums[0] = sum_done(0)
            elimination_begin(sums[0], work)
        if EARLY[0] <= c < CHUNKS - 1:
            eliminate(work.at[0], *share(c - EARLY[0], CHUNKS - EARLY[0]))

    sum_start(1, gram_ref[...] + 0.5 * (cross_ref[...] + cross_ref[...].T))
    adjoint_near(0, per * 2)
    sum_spread(1)
    send_range(1, EARLY[1], CHUNKS)
    adjoint_near(per * 2, n)
    gram_clear()
    eliminate(work.at[0], share(CHUNKS - 1 - EARLY[0], CHUNKS - EARLY[0])[0], rhs)
    inverse0[...] = elimination_end(sums[0], work)

    def second(c):
        arrive(1, c)

        @pl.loop(0, per)
        def _(j):
            s = c * per + j
            value = acc[s]
            for d in range(4):
                value = value + u_in[d, s].astype(f32)
            normal[s] = value
            rounded[s] = value.astype(bf16)

    def third(c):
        value, high = normal[sites(c)], rounded[sites(c)]
        here = r[sites(c)].astype(f32) - times(high, (value - high.astype(f32)).astype(bf16), 0)
        residual[sites(c)] = here
        gram_add(*split(here))

    ahead = CHUNKS - 2
    for c in range(ahead):
        second(c)
        if c < EARLY[2]:
            send(2, c)
        if c == 0:
            sum_gather(1)
            sums[1] = sum_done(1)
            elimination_begin(sums[1], work)
        eliminate(work.at[0], *share(c, ahead))
    keep(0, solved(sums[1], elimination_end(sums[1], work), sums[0]))

    @pl.loop(0, ahead)
    def _(c):
        third(c)

    @pl.loop(ahead, CHUNKS)
    def _(c):
        second(c)
        third(c)

    sum_start(2, gram_ref[...] + cross_ref[...] + cross_ref[...].T)
    apply_near(rounded, lambda s: normal[s], 0, per * 2)
    sum_spread(2)
    send_range(2, EARLY[2], CHUNKS)
    apply_near(rounded, lambda s: normal[s], per * 2, n)
    gram_clear()
    @pl.loop(0, CHUNKS)
    def _(c):
        for copy in copies(1, c):
            copy.wait_send()

    def fourth(c):
        arrive(2, c)

        @pl.loop(0, per)
        def _(j):
            s = c * per + j
            acc[s] = apply_far(s, halo3)

        here = (full[sites(c)] - times(*split(acc[sites(c)]), 0)).astype(bf16)
        gram_ref[...] += gram(here, here)

    def fifth(c):
        normal[sites(c)] = source_times(c, 0)
        high, low = split(residual[sites(c)] + source_times(c, 1))
        u_out[0, sites(c)] = high
        u_out[1, sites(c)] = low

    outs = [pltpu.make_async_copy(source, target, local_sem.at[2 + k]) for k, (source, target) in enumerate(
        ((normal, first_ref), (u_out.at[0], high_ref), (u_out.at[1], low_ref)))]
    begin = EARLY[2] + 1
    for c in range(CHUNKS):
        fourth(c)
        if c == EARLY[2] - 1:
            sum_gather(2)
        if c == EARLY[2]:
            fresh_ref[...] = sum_done(2)
            beta = solved(sums[0], inverse0[...], fresh_ref[...])
            keep(1, beta)
            curvature_ref[...] = dot_t(beta, dot(sums[1], beta))
        if begin <= c < CHUNKS - 1:
            lo, hi = share(c - begin, CHUNKS - 1 - begin, CHUNKS)
            pl.loop(lo, hi)(fifth)
        if c == CHUNKS - 2:
            for copy in outs:
                copy.start()

    sum_start(3, gram_ref[...])
    sum_spread(3)
    sum_gather(3)
    for copy in outs:
        copy.wait()
    for stage in (0, 2):
        @pl.loop(0, CHUNKS)
        def _(c):
            for copy in copies(stage, c):
                copy.wait_send()
    curvature = sum_done(3) - curvature_ref[...]
    curvature_ref[...] = 0.5 * (curvature + curvature.T)
    for k in range(SUMS):
        sum_waits(k)


def krylov(sources, links, sizes):
    ny, nt, nx, nz, comp, rhs = sources.shape
    assert nt == 1 and nx == 1
    n = ny * nz
    n_ta, n_xy = sizes["ta"], sizes["xy"]
    rows = piece_rows(rhs, n_ta)
    anywhere = pl.BlockSpec(memory_space=pl.ANY)
    vmem = pl.BlockSpec(memory_space=pltpu.VMEM)
    slab = lambda *lead: pltpu.VMEM(lead + (n, comp, rhs), bf16)
    wide = pltpu.VMEM((n, comp, rhs), f32)
    pieces = lambda count: pltpu.VMEM((SUMS, count, rows, rhs // 2), f32)
    most = max(n_ta, n_xy)
    square = lambda *lead: pltpu.VMEM(lead + (rhs, rhs), f32)
    return pl.pallas_call(
        functools.partial(krylov_kernel, sizes, ny, nz),
        out_shape=[jax.ShapeDtypeStruct((n, comp, rhs), d) for d in (f32, bf16, bf16)]
        + [jax.ShapeDtypeStruct((rhs, rhs), f32)] * 2,
        in_specs=[anywhere, anywhere],
        out_specs=[anywhere] * 3 + [vmem] * 2,
        scratch_shapes=[
            slab(), pltpu.VMEM((links.shape[0], n, comp, comp), bf16), slab(4), slab(4), slab(4), slab(4), slab(), slab(),
            wide, wide, wide, wide, square(), square(), square(2), square(), square(2), pltpu.VMEM((4, rhs, rhs), bf16),
            pieces(n_ta), pieces(n_ta), pltpu.VMEM((SUMS, rows, rhs // 2), f32), pieces(n_xy), pieces(n_ta),
            pltpu.SemaphoreType.DMA((5,)), pltpu.SemaphoreType.DMA((3, 4, CHUNKS)), pltpu.SemaphoreType.DMA((3, 4, CHUNKS)),
            pltpu.SemaphoreType.DMA((SUMS, 3, most)), pltpu.SemaphoreType.DMA((SUMS, 3, most)),
        ],
        cost_estimate=pl.CostEstimate(flops=int(6e9), bytes_accessed=64 << 20, transcendentals=0),
        compiler_params=pltpu.CompilerParams(collective_id=0, has_side_effects=True, vmem_limit_bytes=67043328),
    )(sources.reshape(n, comp, rhs), links.reshape(links.shape[0], n, comp, comp))


dot = functools.partial(jnp.dot, precision=HI, preferred_element_type=f32)


def dot_t(a, b):
    return lax.dot_general(a, b, TURNED, precision=HI, preferred_element_type=f32)


def split(value):
    high = value.astype(bf16)
    return high, (value - high.astype(f32)).astype(bf16)


def scaled(a):
    row, col = iotas(a.shape[0])
    eye = jnp.where(row == col, 1.0, 0.0).astype(f32)
    diag = a * eye
    down = lax.rsqrt(jnp.sum(diag, axis=1, keepdims=True))
    across = lax.rsqrt(jnp.sum(diag, axis=0, keepdims=True))
    return a * down * across, eye, down, across


def eliminate(x_ref, lo, hi):
    row, col = iotas(x_ref.shape[0])

    def step(k, carry):
        m = x_ref[...]
        pivot_row = x_ref[pl.ds(k, 1), :]
        here = col == k
        pivot_col = jnp.sum(jnp.where(here, m, 0.0), axis=1, keepdims=True)
        hit = here[:1]
        inv = 1.0 / jnp.sum(jnp.where(hit, pivot_row, 0.0), axis=1, keepdims=True)
        line = jnp.where(hit, inv, pivot_row * inv)
        m = jnp.where(here, 0.0, m) - pivot_col * line
        x_ref[...] = jnp.where(row == k, line, m)
        return carry

    lax.fori_loop(lo, hi, step, 0)


def elimination_begin(a, work):
    work[0] = work[1] = scaled(a)[0]


def elimination_end(a, work):
    _, eye, down, across = scaled(a)
    return refined(work[1], work[0], eye, down, across)


def refined(a, x, eye, down, across):
    x = x + dot(x, eye - dot(a, x))
    return x * down * across


def solved(a, inverse, right):
    out = dot(inverse, right)
    return out + dot(inverse, right - dot(a, out))


def solve(a, right, x_ref, s_ref, out_ref):
    s, eye, down, across = scaled(a)
    power = eye - s
    near = power.astype(bf16)
    square = mul(near, near, STRAIGHT)
    near2 = square.astype(bf16)
    fourth = mul(near2, near2, STRAIGHT).astype(bf16)
    inverse = eye + power + square + mul(near, near2, STRAIGHT)
    inverse = (inverse + mul(inverse.astype(bf16), fourth, STRAIGHT)).astype(bf16)
    off = jnp.abs(eye - mul(s.astype(bf16), inverse, STRAIGHT))
    worst = jnp.max(jnp.sum(off, axis=1, keepdims=True))
    right = right * down
    x = mul(inverse, right.astype(bf16), STRAIGHT)
    for _ in range(2):
        x = x + mul(inverse, (right - dot(s, x)).astype(bf16), STRAIGHT)
    out_ref[...] = x * down

    @pl.when(jnp.logical_not(worst < 0.05))
    def _():
        s_ref[...] = s
        x_ref[...] = s
        eliminate(x_ref, 0, a.shape[0])
        x = refined(s_ref[...], x_ref[...], eye, 1.0, 1.0)
        out_ref[...] = solved(s_ref[...], x, right) * down


def closing_kernel(chunks, curvature_ref, fresh_ref, first_hbm, high_hbm, low_hbm, out_hbm,
                   first, high, low, coef, x_ref, s_ref, alpha_ref, load_sem, store_sem):
    n, comp, rhs = first.shape
    per = n // chunks
    loads = [pltpu.make_async_copy(source, target, load_sem.at[k]) for k, (source, target) in enumerate(
        ((first_hbm, first), (high_hbm, high), (low_hbm, low)))]
    for copy in loads:
        copy.start()
    solve(curvature_ref[...], fresh_ref[...], x_ref, s_ref, alpha_ref)
    coef[0], coef[1] = split(alpha_ref[...])
    for copy in loads:
        copy.wait()

    def store(c):
        return pltpu.make_async_copy(first.at[pl.ds(c * per, per)], out_hbm.at[pl.ds(c * per, per)], store_sem.at[c])

    @pl.loop(0, chunks)
    def _(c):
        here = pl.ds(c * per, per)
        left, rest = high[here].reshape(-1, rhs), low[here].reshape(-1, rhs)
        step = mul(left, coef[0], STRAIGHT) + mul(left, coef[1], STRAIGHT) + mul(rest, coef[0], STRAIGHT)
        first[here] = first[here] + step.reshape(per, comp, rhs)
        store(c).start()

    @pl.loop(0, chunks)
    def _(c):
        store(c).wait()


def closing(first, high, low, curvature, fresh):
    vmem, anywhere = pl.BlockSpec(memory_space=pltpu.VMEM), pl.BlockSpec(memory_space=pl.ANY)
    rhs = fresh.shape[0]
    return pl.pallas_call(
        functools.partial(closing_kernel, CHUNKS),
        out_shape=jax.ShapeDtypeStruct(first.shape, f32),
        in_specs=[vmem] * 2 + [anywhere] * 3,
        out_specs=anywhere,
        scratch_shapes=[pltpu.VMEM(first.shape, f32), pltpu.VMEM(first.shape, bf16), pltpu.VMEM(first.shape, bf16),
                        pltpu.VMEM((2, rhs, rhs), bf16)] + [pltpu.VMEM((rhs, rhs), f32)] * 3
        + [pltpu.SemaphoreType.DMA((3,)), pltpu.SemaphoreType.DMA((CHUNKS,))],
        cost_estimate=pl.CostEstimate(flops=int(4e9), bytes_accessed=10 << 20, transcendentals=0),
    )(curvature, fresh, first, high, low)


def solution(mesh):
    sizes = {axis: mesh.shape[axis] for axis in ("ta", "xy")}

    def body(sources, links):
        return closing(*krylov(sources, links, sizes)).reshape(sources.shape)

    return jax.shard_map(
        body,
        mesh=mesh,
        in_specs=(
            P("groups", "ta", "xy", None, None, None),
            P("groups", None, "ta", "xy", None, None, None),
        ),
        out_specs=P("groups", "ta", "xy", None, None, None),
        check_vma=False,
    )
```

```python
import functools

import jax
import jax.numpy as jnp
from jax import lax
from jax.experimental import pallas as pl
from jax.experimental.pallas import tpu as pltpu
from jax.sharding import PartitionSpec as P

mass_term = 2.0
MESH = pl.DeviceIdType.MESH
HI = lax.Precision.HIGHEST
f32 = jnp.float32
bf16 = jnp.bfloat16

HOPS = (("ta", 1), ("ta", -1), ("xy", 1), ("xy", -1))
CHUNKS = 8
EARLY = (2, 3, 4)
SUMS = 4
PARTS = 3

mul = functools.partial(lax.dot_general, preferred_element_type=f32)
STRAIGHT = (((1,), (0,)), ((), ()))
TURNED = (((0,), (0,)), ((), ()))


def iotas(n):
    return lax.broadcasted_iota(jnp.int32, (n, n), 0), lax.broadcasted_iota(jnp.int32, (n, n), 1)


def piece_rows(rhs, n_ta):
    return -(-(rhs + 1) // (8 * n_ta)) * 8


def krylov_kernel(sizes, ny, nz, src, links, first_ref, second_ref, high_ref, low_ref, curvature_ref, fresh_ref,
                  r, lk, halo, u_out, u_in, image, rounded, acc, full, normal, gram_ref, cross_ref, work, inverse0,
                  sums, coef, packed, parts, total, planes, whole, local_sem, bulk_send, bulk_recv, sum_send, sum_recv):
    n_ta, n_xy = sizes["ta"], sizes["xy"]
    me = {axis: lax.axis_index(axis) for axis in sizes}
    n, comp, rhs = r.shape
    per = n // CHUNKS
    half = rhs // 2
    rows = piece_rows(rhs, n_ta)

    def peer(axis, off):
        return lax.rem(me[axis] + off + sizes[axis], sizes[axis])

    def sites(c):
        return pl.ds(c * per, per)

    def vector_copy(stage, d, c, source, halo):
        axis, step = HOPS[d]
        return pltpu.make_async_remote_copy(
            src_ref=source.at[sites(c)], dst_ref=halo.at[d, sites(c)],
            send_sem=bulk_send.at[stage, d, c], recv_sem=bulk_recv.at[stage, d, c],
            device_id={axis: peer(axis, -step)}, device_id_type=MESH)

    def product_copy(d, c):
        axis, step = HOPS[d]
        return pltpu.make_async_remote_copy(
            src_ref=u_out.at[d, sites(c)], dst_ref=u_in.at[d, sites(c)],
            send_sem=bulk_send.at[1, d, c], recv_sem=bulk_recv.at[1, d, c],
            device_id={axis: peer(axis, step)}, device_id_type=MESH)

    def copies(stage, c):
        if stage == 0:
            return [vector_copy(0, d, c, src, halo) for d in (3, 2, 1, 0)]
        if stage == 1:
            return [product_copy(d, c) for d in (3, 2, 1, 0)]
        return [vector_copy(2, d, c, rounded, halo) for d in (3, 2, 1, 0)]

    def send(stage, c):
        for copy in copies(stage, c):
            copy.start()

    def send_range(stage, lo, hi):
        @pl.loop(lo, hi)
        def _(c):
            send(stage, c)

    def arrive(stage, c):
        for copy in copies(stage, c):
            copy.wait_recv()

    tiles = rows // 8
    parts_of = [pl.ds(8 * (tiles * p // PARTS), 8 * (tiles * (p + 1) // PARTS - tiles * p // PARTS)) for p in range(PARTS)]

    def sum_copy(k, stage, p, off, axis, source, target):
        return pltpu.make_async_remote_copy(
            src_ref=source.at[parts_of[p]], dst_ref=target.at[parts_of[p]], send_sem=sum_send.at[k, stage, p, off],
            recv_sem=sum_recv.at[k, stage, p, off], device_id={axis: peer(axis, off)}, device_id_type=MESH)

    def scatter(k, p, off):
        return sum_copy(k, 0, p, off, "ta", packed.at[k, peer("ta", off)], parts.at[k, off])

    def spread(k, p, off):
        return sum_copy(k, 1, p, off, "xy", total.at[k], planes.at[k, me["xy"]])

    def gather(k, p, off):
        return sum_copy(k, 2, p, off, "ta", whole.at[k, me["ta"]], whole.at[k, me["ta"]])

    def came(k, stage, p, off, ref):
        sum_copy(k, stage, p, off, ("ta", "xy", "ta")[stage], ref, ref).wait_recv()

    def sum_start(k, matrix):
        row, col = iotas(half)
        last = matrix[half:, half:]
        mixed = jnp.where(row >= col, matrix[:half, :half], last)
        diag = jnp.sum(jnp.where(row == col, last, 0.0), axis=0, keepdims=True)
        tail = jnp.broadcast_to(diag, (n_ta * rows - rhs, half))
        flat = jnp.concatenate([mixed, matrix[half:, :half], tail], axis=0)
        for i in range(n_ta):
            packed[k, i] = flat[i * rows:(i + 1) * rows]
        for p in range(PARTS):
            for off in range(1, n_ta):
                scatter(k, p, off).start()

    def sum_spread(k):
        for p, here in enumerate(parts_of):
            value = packed[k, me["ta"], here]
            for off in range(1, n_ta):
                came(k, 0, p, off, parts.at[k, off])
                value = value + parts[k, off, here]
            total[k, here] = value
            for off in range(1, n_xy):
                spread(k, p, off).start()

    def sum_gather(k):
        for p, here in enumerate(parts_of):
            for off in range(1, n_xy):
                came(k, 1, p, off, planes.at[k, peer("xy", -off)])
            planes[k, me["xy"], here] = total[k, here]
            value = planes[k, 0, here]
            for i in range(1, n_xy):
                value = value + planes[k, i, here]
            whole[k, me["ta"], here] = value
            for off in range(1, n_ta):
                gather(k, p, off).start()

    def sum_done(k):
        for p in range(PARTS):
            for off in range(1, n_ta):
                came(k, 2, p, off, whole.at[k, peer("ta", -off)])
        flat = jnp.concatenate([whole[k, i] for i in range(n_ta)], axis=0)
        row, col = iotas(half)
        mixed, low = flat[:half], flat[half:rhs]
        turned = mixed.T
        first = jnp.where(row >= col, mixed, turned)
        last = jnp.where(row < col, mixed, turned)
        last = jnp.where(row == col, flat[rhs:rhs + 1], last)
        return jnp.concatenate([jnp.concatenate([first, low.T], axis=1),
                                jnp.concatenate([low, last], axis=1)], axis=0)

    def sum_waits(k):
        for p in range(PARTS):
            for off in range(1, n_ta):
                scatter(k, p, off).wait_send()
                gather(k, p, off).wait_send()
            for off in range(1, n_xy):
                spread(k, p, off).wait_send()

    def gram(a, b):
        a, b = (v.reshape(-1, rhs) for v in (a, b))
        return mul(a, b, TURNED)

    def near(s):
        y, z = s // nz, lax.rem(s, nz)
        at = lambda i, j: lax.rem(i + ny, ny) * nz + lax.rem(j + nz, nz)
        return at(y + 1, z), at(y - 1, z), at(y, z + 1), at(y, z - 1)

    def apply_near(vector, value, lo, hi):
        @pl.loop(lo, hi)
        def _(s):
            total = mass_term * value(s) + mul(lk[0, s], vector[s], STRAIGHT)
            for k, other in enumerate(near(s)):
                total = total + mul(lk[k + 5, s], vector[other], STRAIGHT)
            acc[s] = total

    def apply_far(s, halo):
        total = acc[s]
        for d in range(4):
            total = total + mul(lk[d + 1, s], halo[d, s], STRAIGHT)
        return total

    def adjoint_near(lo, hi):
        @pl.loop(lo, hi)
        def _(s):
            here = image[s]
            total = mass_term * here.astype(f32) + mul(lk[0, s], here, TURNED)
            plus_y, minus_y, plus_z, minus_z = near(s)
            for k, origin in enumerate((minus_y, plus_y, minus_z, plus_z)):
                total = total + mul(lk[k + 5, origin], image[origin], TURNED).astype(bf16).astype(f32)
            acc[s] = total

    loads = [pltpu.make_async_copy(src, r, local_sem.at[0]), pltpu.make_async_copy(links, lk, local_sem.at[1])]
    for copy in loads:
        copy.start()
    barrier = pltpu.get_barrier_semaphore()
    for axis in ("ta", "xy"):
        for off in range(1, sizes[axis]):
            pl.semaphore_signal(barrier, inc=1, device_id={axis: peer(axis, off)}, device_id_type=MESH)
    pl.semaphore_wait(barrier, n_ta + n_xy - 2)

    def gram_add(high, low):
        gram_ref[...] += gram(high, high)
        cross_ref[...] += gram(low, high)

    def gram_clear():
        gram_ref[...] = jnp.zeros((rhs, rhs), f32)
        cross_ref[...] = jnp.zeros((rhs, rhs), f32)

    def times(high, low, k):
        high, low = high.reshape(-1, rhs), low.reshape(-1, rhs)
        out = mul(high, coef[2 * k], STRAIGHT) + mul(high, coef[2 * k + 1], STRAIGHT) + mul(low, coef[2 * k], STRAIGHT)
        return out.reshape(per, comp, rhs)

    def source_times(c, k):
        high = r[sites(c)].reshape(-1, rhs)
        return (mul(high, coef[2 * k], STRAIGHT) + mul(high, coef[2 * k + 1], STRAIGHT)).reshape(per, comp, rhs)

    def keep(k, value):
        high, low = split(value)
        coef[2 * k] = high
        coef[2 * k + 1] = low

    def share(i, count, whole=rhs):
        return whole * i // count, whole * (i + 1) // count

    send_range(0, 0, EARLY[0])
    loads[0].wait()
    sum_start(0, gram(r[...], r[...]))
    loads[1].wait()
    apply_near(r, lambda s: r[s].astype(f32), 0, per * 2)
    sum_spread(0)
    send_range(0, EARLY[0], CHUNKS)
    apply_near(r, lambda s: r[s].astype(f32), per * 2, n)
    gram_clear()
    def first(c):
        arrive(0, c)

        @pl.loop(0, per)
        def _(j):
            s = c * per + j
            value = apply_far(s, halo)
            here, low = split(value)
            full[s] = value
            image[s] = here
            rounded[s] = low
            for d in range(4):
                u_out[d, s] = mul(lk[d + 1, s], here, TURNED).astype(bf16)

        gram_add(image[sites(c)], rounded[sites(c)])

    for c in range(CHUNKS):
        first(c)
        if c < EARLY[1]:
            send(1, c)
        if c == EARLY[0] - 1:
            sum_gather(0)
        if c == EARLY[0]:
            sums[0] = sum_done(0)
            elimination_begin(sums[0], work)
        if EARLY[0] <= c < CHUNKS - 1:
            eliminate(work.at[0], *share(c - EARLY[0], CHUNKS - EARLY[0]))

    sum_start(1, gram_ref[...] + 0.5 * (cross_ref[...] + cross_ref[...].T))
    adjoint_near(0, per * 2)
    sum_spread(1)
    send_range(1, EARLY[1], CHUNKS)
    adjoint_near(per * 2, n)
    gram_clear()
    eliminate(work.at[0], share(CHUNKS - 1 - EARLY[0], CHUNKS - EARLY[0])[0], rhs)
    inverse0[...] = elimination_end(sums[0], work)

    def second(c):
        arrive(1, c)

        @pl.loop(0, per)
        def _(j):
            s = c * per + j
            value = acc[s]
            for d in range(4):
                value = value + u_in[d, s].astype(f32)
            normal[s] = value
            rounded[s] = value.astype(bf16)

    def residual(c):
        value, high = normal[sites(c)], rounded[sites(c)]
        return r[sites(c)].astype(f32) - times(high, (value - high.astype(f32)).astype(bf16), 0)

    def third(c):
        gram_add(*split(residual(c)))

    ahead = CHUNKS - 2
    for c in range(ahead):
        second(c)
        if c < EARLY[2]:
            send(2, c)
        if c == 0:
            sum_gather(1)
            sums[1] = sum_done(1)
            elimination_begin(sums[1], work)
        eliminate(work.at[0], *share(c, ahead))
    keep(0, solved(sums[1], elimination_end(sums[1], work), sums[0]))

    @pl.loop(0, ahead)
    def _(c):
        third(c)

    @pl.loop(ahead, CHUNKS)
    def _(c):
        second(c)
        third(c)

    sum_start(2, gram_ref[...] + cross_ref[...] + cross_ref[...].T)
    apply_near(rounded, lambda s: normal[s], 0, per * 2)
    sum_spread(2)
    send_range(2, EARLY[2], CHUNKS)
    apply_near(rounded, lambda s: normal[s], per * 2, n)
    gram_clear()
    @pl.loop(0, CHUNKS)
    def _(c):
        for copy in copies(1, c):
            copy.wait_send()

    def fourth(c):
        for dirs in ((0, 1), (2,), (3,)) if c == CHUNKS - 1 else ((0, 1, 2, 3),):
            for d in dirs:
                vector_copy(2, d, c, rounded, halo).wait_recv()
            for j in range(per):
                s = c * per + j
                total = acc[s]
                for d in dirs:
                    total = total + mul(lk[d + 1, s], halo[d, s], STRAIGHT)
                acc[s] = total

        here = (full[sites(c)] - times(*split(acc[sites(c)]), 0)).astype(bf16)
        gram_ref[...] += gram(here, here)

    def fifth(c):
        high, low = split(residual(c) + source_times(c, 1))
        u_out[0, sites(c)] = high
        u_out[1, sites(c)] = low
        normal[sites(c)] = source_times(c, 0)

    front, back = pl.ds(0, n // 2), pl.ds(n // 2, n // 2)
    outs = [pltpu.make_async_copy(source, target, local_sem.at[2 + k]) for k, (source, target) in enumerate(
        ((normal.at[front], first_ref), (normal.at[back], second_ref), (u_out.at[0], high_ref), (u_out.at[1], low_ref)))]
    begin = EARLY[2] + 1
    for c in range(CHUNKS):
        fourth(c)
        if c == EARLY[2] - 1:
            sum_gather(2)
        if c == EARLY[2]:
            fresh_ref[...] = sum_done(2)
            beta = solved(sums[0], inverse0[...], fresh_ref[...])
            keep(1, beta)
            curvature_ref[...] = dot_t(beta, dot(sums[1], beta))
        if begin <= c < CHUNKS - 1:
            lo, hi = share(c - begin, CHUNKS - 1 - begin, CHUNKS)
            pl.loop(lo, hi)(fifth)
        if c == CHUNKS - 2:
            for copy in outs:
                copy.start()

    sum_start(3, gram_ref[...])
    sum_spread(3)
    sum_gather(3)
    for copy in outs:
        copy.wait()
    for stage in (0, 2):
        @pl.loop(0, CHUNKS)
        def _(c):
            for copy in copies(stage, c):
                copy.wait_send()
    curvature = sum_done(3) - curvature_ref[...]
    curvature_ref[...] = 0.5 * (curvature + curvature.T)
    for k in range(SUMS):
        sum_waits(k)


def krylov(sources, links, sizes):
    ny, nt, nx, nz, comp, rhs = sources.shape
    assert nt == 1 and nx == 1
    n = ny * nz
    n_ta, n_xy = sizes["ta"], sizes["xy"]
    rows = piece_rows(rhs, n_ta)
    anywhere = pl.BlockSpec(memory_space=pl.ANY)
    vmem = pl.BlockSpec(memory_space=pltpu.VMEM)
    slab = lambda *lead: pltpu.VMEM(lead + (n, comp, rhs), bf16)
    wide = pltpu.VMEM((n, comp, rhs), f32)
    pieces = lambda count: pltpu.VMEM((SUMS, count, rows, rhs // 2), f32)
    most = max(n_ta, n_xy)
    square = lambda *lead: pltpu.VMEM(lead + (rhs, rhs), f32)
    return pl.pallas_call(
        functools.partial(krylov_kernel, sizes, ny, nz),
        out_shape=[jax.ShapeDtypeStruct((n // 2, comp, rhs), f32)] * 2 + [jax.ShapeDtypeStruct((n, comp, rhs), bf16)] * 2
        + [jax.ShapeDtypeStruct((rhs, rhs), f32)] * 2,
        in_specs=[anywhere, anywhere],
        out_specs=[anywhere] * 4 + [vmem] * 2,
        scratch_shapes=[
            slab(), pltpu.VMEM((links.shape[0], n, comp, comp), bf16), slab(4), slab(4), slab(4), slab(), slab(),
            wide, wide, wide, square(), square(), square(2), square(), square(2), pltpu.VMEM((4, rhs, rhs), bf16),
            pieces(n_ta), pieces(n_ta), pltpu.VMEM((SUMS, rows, rhs // 2), f32), pieces(n_xy), pieces(n_ta),
            pltpu.SemaphoreType.DMA((6,)), pltpu.SemaphoreType.DMA((3, 4, CHUNKS)), pltpu.SemaphoreType.DMA((3, 4, CHUNKS)),
            pltpu.SemaphoreType.DMA((SUMS, 3, PARTS, most)), pltpu.SemaphoreType.DMA((SUMS, 3, PARTS, most)),
        ],
        cost_estimate=pl.CostEstimate(flops=int(6e9), bytes_accessed=64 << 20, transcendentals=0),
        compiler_params=pltpu.CompilerParams(collective_id=0, has_side_effects=True, vmem_limit_bytes=46 << 20),
    )(sources.reshape(n, comp, rhs), links.reshape(links.shape[0], n, comp, comp))


dot = functools.partial(jnp.dot, precision=HI, preferred_element_type=f32)


def dot_t(a, b):
    return lax.dot_general(a, b, TURNED, precision=HI, preferred_element_type=f32)


def split(value):
    high = value.astype(bf16)
    return high, (value - high.astype(f32)).astype(bf16)


def scaled(a):
    row, col = iotas(a.shape[0])
    eye = jnp.where(row == col, 1.0, 0.0).astype(f32)
    diag = a * eye
    down = lax.rsqrt(jnp.sum(diag, axis=1, keepdims=True))
    across = lax.rsqrt(jnp.sum(diag, axis=0, keepdims=True))
    return a * down * across, eye, down, across


def eliminate(x_ref, lo, hi):
    row, col = iotas(x_ref.shape[0])

    def step(k, carry):
        m = x_ref[...]
        pivot_row = x_ref[pl.ds(k, 1), :]
        here = col == k
        pivot_col = jnp.sum(jnp.where(here, m, 0.0), axis=1, keepdims=True)
        hit = here[:1]
        inv = 1.0 / jnp.sum(jnp.where(hit, pivot_row, 0.0), axis=1, keepdims=True)
        line = jnp.where(hit, inv, pivot_row * inv)
        m = jnp.where(here, 0.0, m) - pivot_col * line
        x_ref[...] = jnp.where(row == k, line, m)
        return carry

    lax.fori_loop(lo, hi, step, 0)


def elimination_begin(a, work):
    work[0] = work[1] = scaled(a)[0]


def elimination_end(a, work):
    _, eye, down, across = scaled(a)
    return refined(work[1], work[0], eye, down, across)


def refined(a, x, eye, down, across):
    x = x + dot(x, eye - dot(a, x))
    return x * down * across


def solved(a, inverse, right):
    out = dot(inverse, right)
    return out + dot(inverse, right - dot(a, out))


def solve(a, right, x_ref, s_ref, out_ref):
    s, eye, down, across = scaled(a)
    power = eye - s
    near = power.astype(bf16)
    square = mul(near, near, STRAIGHT)
    near2 = square.astype(bf16)
    fourth = mul(near2, near2, STRAIGHT).astype(bf16)
    inverse = eye + power + square + mul(near, near2, STRAIGHT)
    inverse = (inverse + mul(inverse.astype(bf16), fourth, STRAIGHT)).astype(bf16)
    off = jnp.abs(eye - mul(s.astype(bf16), inverse, STRAIGHT))
    worst = jnp.max(jnp.sum(off, axis=1, keepdims=True))
    right = right * down
    x = mul(inverse, right.astype(bf16), STRAIGHT)
    for _ in range(2):
        x = x + mul(inverse, (right - dot(s, x)).astype(bf16), STRAIGHT)
    out_ref[...] = x * down

    @pl.when(jnp.logical_not(worst < 0.05))
    def _():
        s_ref[...] = s
        x_ref[...] = s
        eliminate(x_ref, 0, a.shape[0])
        x = refined(s_ref[...], x_ref[...], eye, 1.0, 1.0)
        out_ref[...] = solved(s_ref[...], x, right) * down


def closing_kernel(chunks, curvature_ref, fresh_ref, first, second, high, low, out_hbm, out, coef, x_ref, s_ref, alpha_ref, store_sem):
    n, comp, rhs = high.shape
    per = n // chunks
    solve(curvature_ref[...], fresh_ref[...], x_ref, s_ref, alpha_ref)
    coef[0], coef[1] = split(alpha_ref[...])

    def store(c):
        return pltpu.make_async_copy(out.at[pl.ds(c * per, per)], out_hbm.at[pl.ds(c * per, per)], store_sem.at[c])

    for base, lo in ((first, 0), (second, chunks // 2)):
        @pl.loop(0, chunks // 2)
        def _(c):
            here = pl.ds((lo + c) * per, per)
            left, rest = high[here].reshape(-1, rhs), low[here].reshape(-1, rhs)
            step = mul(left, coef[0], STRAIGHT) + mul(left, coef[1], STRAIGHT) + mul(rest, coef[0], STRAIGHT)
            out[here] = base[pl.ds(c * per, per)] + step.reshape(per, comp, rhs)
            store(lo + c).start()

    @pl.loop(0, chunks)
    def _(c):
        store(c).wait()


def closing(first, second, high, low, curvature, fresh):
    vmem, anywhere = pl.BlockSpec(memory_space=pltpu.VMEM), pl.BlockSpec(memory_space=pl.ANY)
    rhs = fresh.shape[0]
    return pl.pallas_call(
        functools.partial(closing_kernel, CHUNKS),
        out_shape=jax.ShapeDtypeStruct(high.shape, f32),
        in_specs=[vmem] * 6,
        out_specs=anywhere,
        scratch_shapes=[pltpu.VMEM(high.shape, f32), pltpu.VMEM((2, rhs, rhs), bf16)] + [pltpu.VMEM((rhs, rhs), f32)] * 3
        + [pltpu.SemaphoreType.DMA((CHUNKS,))],
        cost_estimate=pl.CostEstimate(flops=int(4e9), bytes_accessed=10 << 20, transcendentals=0),
        compiler_params=pltpu.CompilerParams(vmem_limit_bytes=20 << 20),
    )(curvature, fresh, first, second, high, low)


def solution(mesh):
    sizes = {axis: mesh.shape[axis] for axis in ("ta", "xy")}

    def body(sources, links):
        return closing(*krylov(sources, links, sizes)).reshape(sources.shape)

    return jax.shard_map(
        body,
        mesh=mesh,
        in_specs=(
            P("groups", "ta", "xy", None, None, None),
            P("groups", None, "ta", "xy", None, None, None),
        ),
        out_specs=P("groups", "ta", "xy", None, None, None),
        check_vma=False,
    )
```

```python
import functools

import jax
import jax.numpy as jnp
from jax import lax
from jax.experimental import pallas as pl
from jax.experimental.pallas import tpu as pltpu
from jax.sharding import PartitionSpec as P

mass_term = 2.0
MESH = pl.DeviceIdType.MESH
HI = lax.Precision.HIGHEST
f32 = jnp.float32
bf16 = jnp.bfloat16

HOPS = (("ta", 1), ("ta", -1), ("xy", 1), ("xy", -1))
CHUNKS = 8
EARLY = (2, 3, 4)
SUMS = 4
PARTS = 1

mul = functools.partial(lax.dot_general, preferred_element_type=f32)
STRAIGHT = (((1,), (0,)), ((), ()))
TURNED = (((0,), (0,)), ((), ()))


def iotas(n):
    return lax.broadcasted_iota(jnp.int32, (n, n), 0), lax.broadcasted_iota(jnp.int32, (n, n), 1)


def piece_rows(rhs, n_ta):
    return -(-(rhs + 1) // (8 * n_ta)) * 8


def krylov_kernel(sizes, ny, nz, src, links, first_ref, second_ref, high_ref, low_ref, curvature_ref, fresh_ref,
                  r, lk, halo, u_out, u_in, image, rounded, acc, full, normal, gram_ref, cross_ref, work, inverse0,
                  sums, coef, packed, parts, total, planes, whole, local_sem, bulk_send, bulk_recv, sum_send, sum_recv):
    n_ta, n_xy = sizes["ta"], sizes["xy"]
    me = {axis: lax.axis_index(axis) for axis in sizes}
    n, comp, rhs = r.shape
    per = n // CHUNKS
    half = rhs // 2
    rows = piece_rows(rhs, n_ta)

    def peer(axis, off):
        return lax.rem(me[axis] + off + sizes[axis], sizes[axis])

    def sites(c):
        return pl.ds(c * per, per)

    def vector_copy(stage, d, c, source, halo):
        axis, step = HOPS[d]
        return pltpu.make_async_remote_copy(
            src_ref=source.at[sites(c)], dst_ref=halo.at[d, sites(c)],
            send_sem=bulk_send.at[stage, d, c], recv_sem=bulk_recv.at[stage, d, c],
            device_id={axis: peer(axis, -step)}, device_id_type=MESH)

    def product_copy(d, c):
        axis, step = HOPS[d]
        return pltpu.make_async_remote_copy(
            src_ref=u_out.at[d, sites(c)], dst_ref=u_in.at[d, sites(c)],
            send_sem=bulk_send.at[1, d, c], recv_sem=bulk_recv.at[1, d, c],
            device_id={axis: peer(axis, step)}, device_id_type=MESH)

    def copies(stage, c, dirs=(3, 2, 1, 0)):
        if stage == 1:
            return [product_copy(d, c) for d in dirs]
        return [vector_copy(stage, d, c, rounded if stage else src, halo) for d in dirs]

    def send(stage, c):
        last = (me["xy"] + 1) // n_xy
        first = (2 + last, 3 - last, 2 + last)[stage]
        source, target = ((src, halo), (u_out, u_in), (rounded, halo))[stage]
        for d, step in ((first, 2 * last - 1), (5 - first, 1 - 2 * last)):
            pltpu.make_async_remote_copy(
                src_ref=source.at[d, sites(c)] if stage == 1 else source.at[sites(c)], dst_ref=target.at[d, sites(c)],
                send_sem=bulk_send.at[stage, d, c], recv_sem=bulk_recv.at[stage, d, c],
                device_id={"xy": peer("xy", step)}, device_id_type=MESH).start()
        for copy in copies(stage, c, (1, 0)):
            copy.start()

    def send_range(stage, lo, hi):
        @pl.loop(lo, hi)
        def _(c):
            send(stage, c)

    def arrive(stage, c):
        for copy in copies(stage, c):
            copy.wait_recv()

    tiles = rows // 8
    parts_of = [pl.ds(8 * (tiles * p // PARTS), 8 * (tiles * (p + 1) // PARTS - tiles * p // PARTS)) for p in range(PARTS)]

    def sum_copy(k, stage, p, off, axis, source, target):
        return pltpu.make_async_remote_copy(
            src_ref=source.at[parts_of[p]], dst_ref=target.at[parts_of[p]], send_sem=sum_send.at[k, stage, p, off],
            recv_sem=sum_recv.at[k, stage, p, off], device_id={axis: peer(axis, off)}, device_id_type=MESH)

    def scatter(k, p, off):
        return sum_copy(k, 0, p, off, "ta", packed.at[k, peer("ta", off)], parts.at[k, off])

    def spread(k, p, off):
        return sum_copy(k, 1, p, off, "xy", total.at[k], planes.at[k, me["xy"]])

    def gather(k, p, off):
        return sum_copy(k, 2, p, off, "ta", whole.at[k, me["ta"]], whole.at[k, me["ta"]])

    def came(k, stage, p, off, ref):
        sum_copy(k, stage, p, off, ("ta", "xy", "ta")[stage], ref, ref).wait_recv()

    def sum_start(k, matrix):
        row, col = iotas(half)
        last = matrix[half:, half:]
        mixed = jnp.where(row >= col, matrix[:half, :half], last)
        diag = jnp.sum(jnp.where(row == col, last, 0.0), axis=0, keepdims=True)
        tail = jnp.broadcast_to(diag, (n_ta * rows - rhs, half))
        flat = jnp.concatenate([mixed, matrix[half:, :half], tail], axis=0)
        for i in range(n_ta):
            packed[k, i] = flat[i * rows:(i + 1) * rows]
        for p in range(PARTS):
            for off in range(1, n_ta):
                scatter(k, p, off).start()

    def sum_spread(k):
        for p, here in enumerate(parts_of):
            value = packed[k, me["ta"], here]
            for off in range(1, n_ta):
                came(k, 0, p, off, parts.at[k, off])
                value = value + parts[k, off, here]
            total[k, here] = value
            for off in range(1, n_xy):
                spread(k, p, off).start()

    def sum_gather(k):
        for p, here in enumerate(parts_of):
            for off in range(1, n_xy):
                came(k, 1, p, off, planes.at[k, peer("xy", -off)])
            planes[k, me["xy"], here] = total[k, here]
            value = planes[k, 0, here]
            for i in range(1, n_xy):
                value = value + planes[k, i, here]
            whole[k, me["ta"], here] = value
            for off in range(1, n_ta):
                gather(k, p, off).start()

    def sum_done(k):
        for p in range(PARTS):
            for off in range(1, n_ta):
                came(k, 2, p, off, whole.at[k, peer("ta", -off)])
        flat = jnp.concatenate([whole[k, i] for i in range(n_ta)], axis=0)
        row, col = iotas(half)
        mixed, low = flat[:half], flat[half:rhs]
        turned = mixed.T
        first = jnp.where(row >= col, mixed, turned)
        last = jnp.where(row < col, mixed, turned)
        last = jnp.where(row == col, flat[rhs:rhs + 1], last)
        return jnp.concatenate([jnp.concatenate([first, low.T], axis=1),
                                jnp.concatenate([low, last], axis=1)], axis=0)

    def sum_waits(k):
        for p in range(PARTS):
            for off in range(1, n_ta):
                scatter(k, p, off).wait_send()
                gather(k, p, off).wait_send()
            for off in range(1, n_xy):
                spread(k, p, off).wait_send()

    def gram(a, b):
        a, b = (v.reshape(-1, rhs) for v in (a, b))
        return mul(a, b, TURNED)

    def near(s):
        y, z = s // nz, lax.rem(s, nz)
        at = lambda i, j: lax.rem(i + ny, ny) * nz + lax.rem(j + nz, nz)
        return at(y + 1, z), at(y - 1, z), at(y, z + 1), at(y, z - 1)

    def apply_near(vector, value, lo, hi):
        @pl.loop(lo, hi)
        def _(s):
            total = mass_term * value(s) + mul(lk[0, s], vector[s], STRAIGHT)
            for k, other in enumerate(near(s)):
                total = total + mul(lk[k + 5, s], vector[other], STRAIGHT)
            acc[s] = total

    def apply_far(s, halo):
        total = acc[s]
        for d in range(4):
            total = total + mul(lk[d + 1, s], halo[d, s], STRAIGHT)
        return total

    def adjoint_near(lo, hi):
        @pl.loop(lo, hi)
        def _(s):
            here = image[s]
            total = mass_term * here.astype(f32) + mul(lk[0, s], here, TURNED)
            plus_y, minus_y, plus_z, minus_z = near(s)
            for k, origin in enumerate((minus_y, plus_y, minus_z, plus_z)):
                total = total + mul(lk[k + 5, origin], image[origin], TURNED).astype(bf16).astype(f32)
            acc[s] = total

    loads = [pltpu.make_async_copy(src, r, local_sem.at[0]), pltpu.make_async_copy(links, lk, local_sem.at[1])]
    for copy in loads:
        copy.start()
    barrier = pltpu.get_barrier_semaphore()
    for axis in ("ta", "xy"):
        for off in range(1, sizes[axis]):
            pl.semaphore_signal(barrier, inc=1, device_id={axis: peer(axis, off)}, device_id_type=MESH)
    pl.semaphore_wait(barrier, n_ta + n_xy - 2)

    def gram_add(high, low):
        gram_ref[...] += gram(high, high)
        cross_ref[...] += gram(low, high)

    def gram_clear():
        gram_ref[...] = jnp.zeros((rhs, rhs), f32)
        cross_ref[...] = jnp.zeros((rhs, rhs), f32)

    def times(high, low, k):
        high, low = high.reshape(-1, rhs), low.reshape(-1, rhs)
        out = mul(high, coef[2 * k], STRAIGHT) + mul(high, coef[2 * k + 1], STRAIGHT) + mul(low, coef[2 * k], STRAIGHT)
        return out.reshape(per, comp, rhs)

    def source_times(c, k):
        high = r[sites(c)].reshape(-1, rhs)
        return (mul(high, coef[2 * k], STRAIGHT) + mul(high, coef[2 * k + 1], STRAIGHT)).reshape(per, comp, rhs)

    def keep(k, value):
        high, low = split(value)
        coef[2 * k] = high
        coef[2 * k + 1] = low

    def share(i, count, whole=rhs):
        return whole * i // count, whole * (i + 1) // count

    send_range(0, 0, EARLY[0])
    loads[0].wait()
    sum_start(0, gram(r[...], r[...]))
    loads[1].wait()
    apply_near(r, lambda s: r[s].astype(f32), 0, per * 2)
    sum_spread(0)
    send_range(0, EARLY[0], CHUNKS)
    apply_near(r, lambda s: r[s].astype(f32), per * 2, n)
    gram_clear()
    def first(c):
        arrive(0, c)

        @pl.loop(0, per)
        def _(j):
            s = c * per + j
            value = apply_far(s, halo)
            here, low = split(value)
            full[s] = value
            image[s] = here
            rounded[s] = low
            for d in range(4):
                u_out[d, s] = mul(lk[d + 1, s], here, TURNED).astype(bf16)

        gram_add(image[sites(c)], rounded[sites(c)])

    for c in range(CHUNKS):
        first(c)
        if c < EARLY[1]:
            send(1, c)
        if c == EARLY[0] - 1:
            sum_gather(0)
        if c == EARLY[0]:
            sums[0] = sum_done(0)
            elimination_begin(sums[0], work)
        if EARLY[0] <= c < CHUNKS - 1:
            eliminate(work.at[0], *share(c - EARLY[0], CHUNKS - EARLY[0]))

    sum_start(1, gram_ref[...] + 0.5 * (cross_ref[...] + cross_ref[...].T))
    adjoint_near(0, per * 2)
    sum_spread(1)
    send_range(1, EARLY[1], CHUNKS)
    adjoint_near(per * 2, n)
    gram_clear()
    eliminate(work.at[0], share(CHUNKS - 1 - EARLY[0], CHUNKS - EARLY[0])[0], rhs)
    inverse0[...] = elimination_end(sums[0], work)

    def second(c):
        arrive(1, c)

        @pl.loop(0, per)
        def _(j):
            s = c * per + j
            value = acc[s]
            for d in range(4):
                value = value + u_in[d, s].astype(f32)
            normal[s] = value
            rounded[s] = value.astype(bf16)

    def residual(c):
        value, high = normal[sites(c)], rounded[sites(c)]
        return r[sites(c)].astype(f32) - times(high, (value - high.astype(f32)).astype(bf16), 0)

    def third(c):
        gram_add(*split(residual(c)))

    ahead = CHUNKS - 2
    for c in range(ahead):
        second(c)
        if c < EARLY[2]:
            send(2, c)
        if c == 0:
            sum_gather(1)
            sums[1] = sum_done(1)
            elimination_begin(sums[1], work)
        eliminate(work.at[0], *share(c, ahead))
    keep(0, solved(sums[1], elimination_end(sums[1], work), sums[0]))

    @pl.loop(0, ahead)
    def _(c):
        third(c)

    @pl.loop(ahead, CHUNKS)
    def _(c):
        second(c)
        third(c)

    sum_start(2, gram_ref[...] + cross_ref[...] + cross_ref[...].T)
    apply_near(rounded, lambda s: normal[s], 0, per * 2)
    sum_spread(2)
    send_range(2, EARLY[2], CHUNKS)
    apply_near(rounded, lambda s: normal[s], per * 2, n)
    gram_clear()
    @pl.loop(0, CHUNKS)
    def _(c):
        for copy in copies(1, c):
            copy.wait_send()

    def fourth(c):
        for dirs in ((0, 1), (2,), (3,)) if c == CHUNKS - 1 else ((0, 1, 2, 3),):
            for d in dirs:
                vector_copy(2, d, c, rounded, halo).wait_recv()
            for j in range(per):
                s = c * per + j
                total = acc[s]
                for d in dirs:
                    total = total + mul(lk[d + 1, s], halo[d, s], STRAIGHT)
                acc[s] = total

        here = (full[sites(c)] - times(*split(acc[sites(c)]), 0)).astype(bf16)
        gram_ref[...] += gram(here, here)

    def fifth(c):
        high, low = split(residual(c) + source_times(c, 1))
        u_out[0, sites(c)] = high
        u_out[1, sites(c)] = low
        normal[sites(c)] = source_times(c, 0)

    front, back = pl.ds(0, n // 2), pl.ds(n // 2, n // 2)
    outs = [pltpu.make_async_copy(source, target, local_sem.at[2 + k]) for k, (source, target) in enumerate(
        ((normal.at[front], first_ref), (normal.at[back], second_ref), (u_out.at[0], high_ref), (u_out.at[1], low_ref)))]
    begin = EARLY[2] + 1
    for c in range(CHUNKS):
        fourth(c)
        if c == EARLY[2] - 1:
            sum_gather(2)
        if c == EARLY[2]:
            fresh_ref[...] = sum_done(2)
            beta = solved(sums[0], inverse0[...], fresh_ref[...])
            keep(1, beta)
            curvature_ref[...] = dot_t(beta, dot(sums[1], beta))
        if begin <= c < CHUNKS - 1:
            lo, hi = share(c - begin, CHUNKS - 1 - begin, CHUNKS)
            pl.loop(lo, hi)(fifth)
        if c == CHUNKS - 2:
            for copy in outs:
                copy.start()

    sum_start(3, gram_ref[...])
    sum_spread(3)
    sum_gather(3)
    for copy in outs:
        copy.wait()
    for stage in (0, 2):
        @pl.loop(0, CHUNKS)
        def _(c):
            for copy in copies(stage, c):
                copy.wait_send()
    curvature = sum_done(3) - curvature_ref[...]
    curvature_ref[...] = 0.5 * (curvature + curvature.T)
    for k in range(SUMS):
        sum_waits(k)


def krylov(sources, links, sizes):
    ny, nt, nx, nz, comp, rhs = sources.shape
    assert nt == 1 and nx == 1
    n = ny * nz
    n_ta, n_xy = sizes["ta"], sizes["xy"]
    rows = piece_rows(rhs, n_ta)
    anywhere = pl.BlockSpec(memory_space=pl.ANY)
    vmem = pl.BlockSpec(memory_space=pltpu.VMEM)
    slab = lambda *lead: pltpu.VMEM(lead + (n, comp, rhs), bf16)
    wide = pltpu.VMEM((n, comp, rhs), f32)
    pieces = lambda count: pltpu.VMEM((SUMS, count, rows, rhs // 2), f32)
    most = max(n_ta, n_xy)
    square = lambda *lead: pltpu.VMEM(lead + (rhs, rhs), f32)
    return pl.pallas_call(
        functools.partial(krylov_kernel, sizes, ny, nz),
        out_shape=[jax.ShapeDtypeStruct((n // 2, comp, rhs), f32)] * 2 + [jax.ShapeDtypeStruct((n, comp, rhs), bf16)] * 2
        + [jax.ShapeDtypeStruct((rhs, rhs), f32)] * 2,
        in_specs=[anywhere, anywhere],
        out_specs=[anywhere] * 4 + [vmem] * 2,
        scratch_shapes=[
            slab(), pltpu.VMEM((links.shape[0], n, comp, comp), bf16), slab(4), slab(4), slab(4), slab(), slab(),
            wide, wide, wide, square(), square(), square(2), square(), square(2), pltpu.VMEM((4, rhs, rhs), bf16),
            pieces(n_ta), pieces(n_ta), pltpu.VMEM((SUMS, rows, rhs // 2), f32), pieces(n_xy), pieces(n_ta),
            pltpu.SemaphoreType.DMA((6,)), pltpu.SemaphoreType.DMA((3, 4, CHUNKS)), pltpu.SemaphoreType.DMA((3, 4, CHUNKS)),
            pltpu.SemaphoreType.DMA((SUMS, 3, PARTS, most)), pltpu.SemaphoreType.DMA((SUMS, 3, PARTS, most)),
        ],
        cost_estimate=pl.CostEstimate(flops=int(6e9), bytes_accessed=64 << 20, transcendentals=0),
        compiler_params=pltpu.CompilerParams(collective_id=0, has_side_effects=True, vmem_limit_bytes=46 << 20),
    )(sources.reshape(n, comp, rhs), links.reshape(links.shape[0], n, comp, comp))


dot = functools.partial(jnp.dot, precision=HI, preferred_element_type=f32)


def dot_t(a, b):
    return lax.dot_general(a, b, TURNED, precision=HI, preferred_element_type=f32)


def split(value):
    high = value.astype(bf16)
    return high, (value - high.astype(f32)).astype(bf16)


def scaled(a):
    row, col = iotas(a.shape[0])
    eye = jnp.where(row == col, 1.0, 0.0).astype(f32)
    diag = a * eye
    down = lax.rsqrt(jnp.sum(diag, axis=1, keepdims=True))
    across = lax.rsqrt(jnp.sum(diag, axis=0, keepdims=True))
    return a * down * across, eye, down, across


def eliminate(x_ref, lo, hi):
    row, col = iotas(x_ref.shape[0])

    def step(k, carry):
        m = x_ref[...]
        pivot_row = x_ref[pl.ds(k, 1), :]
        here = col == k
        pivot_col = jnp.sum(jnp.where(here, m, 0.0), axis=1, keepdims=True)
        hit = here[:1]
        inv = 1.0 / jnp.sum(jnp.where(hit, pivot_row, 0.0), axis=1, keepdims=True)
        line = jnp.where(hit, inv, pivot_row * inv)
        m = jnp.where(here, 0.0, m) - pivot_col * line
        x_ref[...] = jnp.where(row == k, line, m)
        return carry

    lax.fori_loop(lo, hi, step, 0)


def elimination_begin(a, work):
    work[0] = work[1] = scaled(a)[0]


def elimination_end(a, work):
    _, eye, down, across = scaled(a)
    return refined(work[1], work[0], eye, down, across)


def refined(a, x, eye, down, across):
    x = x + dot(x, eye - dot(a, x))
    return x * down * across


def solved(a, inverse, right):
    out = dot(inverse, right)
    return out + dot(inverse, right - dot(a, out))


def solve(a, right, x_ref, s_ref, out_ref):
    s, eye, down, across = scaled(a)
    power = eye - s
    near = power.astype(bf16)
    square = mul(near, near, STRAIGHT)
    near2 = square.astype(bf16)
    fourth = mul(near2, near2, STRAIGHT).astype(bf16)
    inverse = eye + power + square + mul(near, near2, STRAIGHT)
    inverse = (inverse + mul(inverse.astype(bf16), fourth, STRAIGHT)).astype(bf16)
    off = jnp.abs(eye - mul(s.astype(bf16), inverse, STRAIGHT))
    worst = jnp.max(jnp.sum(off, axis=1, keepdims=True))
    right = right * down
    x = mul(inverse, right.astype(bf16), STRAIGHT)
    for _ in range(2):
        x = x + mul(inverse, (right - dot(s, x)).astype(bf16), STRAIGHT)
    out_ref[...] = x * down

    @pl.when(jnp.logical_not(worst < 0.05))
    def _():
        s_ref[...] = s
        x_ref[...] = s
        eliminate(x_ref, 0, a.shape[0])
        x = refined(s_ref[...], x_ref[...], eye, 1.0, 1.0)
        out_ref[...] = solved(s_ref[...], x, right) * down


def closing_kernel(chunks, curvature_ref, fresh_ref, first, second, high, low, out_hbm, out, coef, x_ref, s_ref, alpha_ref, store_sem):
    n, comp, rhs = high.shape
    per = n // chunks
    solve(curvature_ref[...], fresh_ref[...], x_ref, s_ref, alpha_ref)
    coef[0], coef[1] = split(alpha_ref[...])

    def store(c):
        return pltpu.make_async_copy(out.at[pl.ds(c * per, per)], out_hbm.at[pl.ds(c * per, per)], store_sem.at[c])

    for base, lo in ((first, 0), (second, chunks // 2)):
        @pl.loop(0, chunks // 2)
        def _(c):
            here = pl.ds((lo + c) * per, per)
            left, rest = high[here].reshape(-1, rhs), low[here].reshape(-1, rhs)
            step = mul(left, coef[0], STRAIGHT) + mul(left, coef[1], STRAIGHT) + mul(rest, coef[0], STRAIGHT)
            out[here] = base[pl.ds(c * per, per)] + step.reshape(per, comp, rhs)
            store(lo + c).start()

    @pl.loop(0, chunks)
    def _(c):
        store(c).wait()


def closing(first, second, high, low, curvature, fresh):
    vmem, anywhere = pl.BlockSpec(memory_space=pltpu.VMEM), pl.BlockSpec(memory_space=pl.ANY)
    rhs = fresh.shape[0]
    return pl.pallas_call(
        functools.partial(closing_kernel, CHUNKS),
        out_shape=jax.ShapeDtypeStruct(high.shape, f32),
        in_specs=[vmem] * 6,
        out_specs=anywhere,
        scratch_shapes=[pltpu.VMEM(high.shape, f32), pltpu.VMEM((2, rhs, rhs), bf16)] + [pltpu.VMEM((rhs, rhs), f32)] * 3
        + [pltpu.SemaphoreType.DMA((CHUNKS,))],
        cost_estimate=pl.CostEstimate(flops=int(4e9), bytes_accessed=10 << 20, transcendentals=0),
        compiler_params=pltpu.CompilerParams(vmem_limit_bytes=20 << 20),
    )(curvature, fresh, first, second, high, low)


def solution(mesh):
    sizes = {axis: mesh.shape[axis] for axis in ("ta", "xy")}

    def body(sources, links):
        return closing(*krylov(sources, links, sizes)).reshape(sources.shape)

    return jax.shard_map(
        body,
        mesh=mesh,
        in_specs=(
            P("groups", "ta", "xy", None, None, None),
            P("groups", None, "ta", "xy", None, None, None),
        ),
        out_specs=P("groups", "ta", "xy", None, None, None),
        check_vma=False,
    )
```

```python
import functools

import jax
import jax.numpy as jnp
from jax import lax
from jax.experimental import pallas as pl
from jax.experimental.pallas import tpu as pltpu
from jax.sharding import PartitionSpec as P

mass_term = 2.0
MESH = pl.DeviceIdType.MESH
HI = lax.Precision.HIGHEST
f32 = jnp.float32
bf16 = jnp.bfloat16

HOPS = (("ta", 1), ("ta", -1), ("xy", 1), ("xy", -1))
CHUNKS = 8
EARLY = (2, 3, 4)
SUMS = 4
PARTS = 1

mul = functools.partial(lax.dot_general, preferred_element_type=f32)
STRAIGHT = (((1,), (0,)), ((), ()))
TURNED = (((0,), (0,)), ((), ()))


def iotas(n):
    return lax.broadcasted_iota(jnp.int32, (n, n), 0), lax.broadcasted_iota(jnp.int32, (n, n), 1)


def piece_rows(rhs, n_ta):
    return -(-(rhs + 1) // (8 * n_ta)) * 8


def krylov_kernel(sizes, ny, nz, src, links, first_ref, second_ref, high_ref, low_ref, curvature_ref, fresh_ref,
                  r, lk, halo, u_out, u_in, image, rounded, acc, full, normal, gram_ref, cross_ref, work, inverse0,
                  sums, coef, packed, parts, total, planes, whole, local_sem, bulk_send, bulk_recv, sum_send, sum_recv):
    n_ta, n_xy = sizes["ta"], sizes["xy"]
    me = {axis: lax.axis_index(axis) for axis in sizes}
    n, comp, rhs = r.shape
    per = n // CHUNKS
    half = rhs // 2
    rows = piece_rows(rhs, n_ta)

    def peer(axis, off):
        return lax.rem(me[axis] + off + sizes[axis], sizes[axis])

    def sites(c):
        return pl.ds(c * per, per)

    def vector_copy(stage, d, c, source, halo):
        axis, step = HOPS[d]
        return pltpu.make_async_remote_copy(
            src_ref=source.at[sites(c)], dst_ref=halo.at[d, sites(c)],
            send_sem=bulk_send.at[stage, d, c], recv_sem=bulk_recv.at[stage, d, c],
            device_id={axis: peer(axis, -step)}, device_id_type=MESH)

    def product_copy(d, c):
        axis, step = HOPS[d]
        return pltpu.make_async_remote_copy(
            src_ref=u_out.at[d, sites(c)], dst_ref=u_in.at[d, sites(c)],
            send_sem=bulk_send.at[1, d, c], recv_sem=bulk_recv.at[1, d, c],
            device_id={axis: peer(axis, step)}, device_id_type=MESH)

    def copies(stage, c, dirs=(3, 2, 1, 0)):
        if stage == 1:
            return [product_copy(d, c) for d in dirs]
        return [vector_copy(stage, d, c, rounded if stage else src, halo) for d in dirs]

    def send(stage, c):
        last = (me["xy"] + 1) // n_xy
        first = (2 + last, 3 - last, 2 + last)[stage]
        source, target = ((src, halo), (u_out, u_in), (rounded, halo))[stage]
        for d, step in ((first, 2 * last - 1), (5 - first, 1 - 2 * last)):
            pltpu.make_async_remote_copy(
                src_ref=source.at[d, sites(c)] if stage == 1 else source.at[sites(c)], dst_ref=target.at[d, sites(c)],
                send_sem=bulk_send.at[stage, d, c], recv_sem=bulk_recv.at[stage, d, c],
                device_id={"xy": peer("xy", step)}, device_id_type=MESH).start()
        for copy in copies(stage, c, (1, 0)):
            copy.start()

    def send_range(stage, lo, hi):
        @pl.loop(lo, hi)
        def _(c):
            send(stage, c)

    def arrive(stage, c):
        for copy in copies(stage, c):
            copy.wait_recv()

    tiles = rows // 8
    parts_of = [pl.ds(8 * (tiles * p // PARTS), 8 * (tiles * (p + 1) // PARTS - tiles * p // PARTS)) for p in range(PARTS)]

    def sum_copy(k, stage, p, off, axis, source, target):
        return pltpu.make_async_remote_copy(
            src_ref=source.at[parts_of[p]], dst_ref=target.at[parts_of[p]], send_sem=sum_send.at[k, stage, p, off],
            recv_sem=sum_recv.at[k, stage, p, off], device_id={axis: peer(axis, off)}, device_id_type=MESH)

    def scatter(k, p, off):
        return sum_copy(k, 0, p, off, "ta", packed.at[k, peer("ta", off)], parts.at[k, off])

    def spread(k, p, off):
        return sum_copy(k, 1, p, off, "xy", total.at[k], planes.at[k, me["xy"]])

    def gather(k, p, off):
        return sum_copy(k, 2, p, off, "ta", whole.at[k, me["ta"]], whole.at[k, me["ta"]])

    def came(k, stage, p, off, ref):
        sum_copy(k, stage, p, off, ("ta", "xy", "ta")[stage], ref, ref).wait_recv()

    def sum_start(k, matrix):
        row, col = iotas(half)
        last = matrix[half:, half:]
        mixed = jnp.where(row >= col, matrix[:half, :half], last)
        diag = jnp.sum(jnp.where(row == col, last, 0.0), axis=0, keepdims=True)
        tail = jnp.broadcast_to(diag, (n_ta * rows - rhs, half))
        flat = jnp.concatenate([mixed, matrix[half:, :half], tail], axis=0)
        for i in range(n_ta):
            packed[k, i] = flat[i * rows:(i + 1) * rows]
        for p in range(PARTS):
            for off in range(1, n_ta):
                scatter(k, p, off).start()

    def sum_spread(k):
        for p, here in enumerate(parts_of):
            value = packed[k, me["ta"], here]
            for off in range(1, n_ta):
                came(k, 0, p, off, parts.at[k, off])
                value = value + parts[k, off, here]
            total[k, here] = value
            for off in range(1, n_xy):
                spread(k, p, off).start()

    def sum_gather(k):
        for p, here in enumerate(parts_of):
            for off in range(1, n_xy):
                came(k, 1, p, off, planes.at[k, peer("xy", -off)])
            planes[k, me["xy"], here] = total[k, here]
            value = planes[k, 0, here]
            for i in range(1, n_xy):
                value = value + planes[k, i, here]
            whole[k, me["ta"], here] = value
            for off in range(1, n_ta):
                gather(k, p, off).start()

    def sum_done(k):
        for p in range(PARTS):
            for off in range(1, n_ta):
                came(k, 2, p, off, whole.at[k, peer("ta", -off)])
        flat = jnp.concatenate([whole[k, i] for i in range(n_ta)], axis=0)
        row, col = iotas(half)
        mixed, low = flat[:half], flat[half:rhs]
        turned = mixed.T
        first = jnp.where(row >= col, mixed, turned)
        last = jnp.where(row < col, mixed, turned)
        last = jnp.where(row == col, flat[rhs:rhs + 1], last)
        return jnp.concatenate([jnp.concatenate([first, low.T], axis=1),
                                jnp.concatenate([low, last], axis=1)], axis=0)

    def sum_waits(k):
        for p in range(PARTS):
            for off in range(1, n_ta):
                scatter(k, p, off).wait_send()
                gather(k, p, off).wait_send()
            for off in range(1, n_xy):
                spread(k, p, off).wait_send()

    def gram(a, b):
        a, b = (v.reshape(-1, rhs) for v in (a, b))
        return mul(a, b, TURNED)

    def near(s):
        y, z = s // nz, lax.rem(s, nz)
        at = lambda i, j: lax.rem(i + ny, ny) * nz + lax.rem(j + nz, nz)
        return at(y + 1, z), at(y - 1, z), at(y, z + 1), at(y, z - 1)

    def apply_near(vector, value, lo, hi):
        @pl.loop(lo, hi)
        def _(s):
            total = mass_term * value(s) + mul(lk[0, s], vector[s], STRAIGHT)
            for k, other in enumerate(near(s)):
                total = total + mul(lk[k + 5, s], vector[other], STRAIGHT)
            acc[s] = total

    def apply_far(s, halo):
        total = acc[s]
        for d in range(4):
            total = total + mul(lk[d + 1, s], halo[d, s], STRAIGHT)
        return total

    def adjoint_near(lo, hi):
        @pl.loop(lo, hi)
        def _(s):
            here = image[s]
            total = mass_term * here.astype(f32) + mul(lk[0, s], here, TURNED)
            plus_y, minus_y, plus_z, minus_z = near(s)
            for k, origin in enumerate((minus_y, plus_y, minus_z, plus_z)):
                total = total + mul(lk[k + 5, origin], image[origin], TURNED).astype(bf16).astype(f32)
            acc[s] = total

    loads = [pltpu.make_async_copy(src, r, local_sem.at[0]), pltpu.make_async_copy(links, lk, local_sem.at[1])]
    for copy in loads:
        copy.start()
    barrier = pltpu.get_barrier_semaphore()
    for axis in ("ta", "xy"):
        for off in range(1, sizes[axis]):
            pl.semaphore_signal(barrier, inc=1, device_id={axis: peer(axis, off)}, device_id_type=MESH)
    pl.semaphore_wait(barrier, n_ta + n_xy - 2)

    def gram_add(high, low):
        gram_ref[...] += gram(high, high)
        cross_ref[...] += gram(low, high)

    def gram_clear():
        gram_ref[...] = jnp.zeros((rhs, rhs), f32)
        cross_ref[...] = jnp.zeros((rhs, rhs), f32)

    def times(high, low, k):
        high, low = high.reshape(-1, rhs), low.reshape(-1, rhs)
        out = mul(high, coef[2 * k], STRAIGHT) + mul(high, coef[2 * k + 1], STRAIGHT) + mul(low, coef[2 * k], STRAIGHT)
        return out.reshape(per, comp, rhs)

    def source_times(c, k):
        high = r[sites(c)].reshape(-1, rhs)
        return (mul(high, coef[2 * k], STRAIGHT) + mul(high, coef[2 * k + 1], STRAIGHT)).reshape(per, comp, rhs)

    def keep(k, value):
        high, low = split(value)
        coef[2 * k] = high
        coef[2 * k + 1] = low

    def share(i, count, whole=rhs):
        return whole * i // count, whole * (i + 1) // count

    send_range(0, 0, EARLY[0])
    loads[0].wait()
    sum_start(0, gram(r[...], r[...]))
    loads[1].wait()
    apply_near(r, lambda s: r[s].astype(f32), 0, per * 2)
    sum_spread(0)
    send_range(0, EARLY[0], CHUNKS)
    apply_near(r, lambda s: r[s].astype(f32), per * 2, n)
    gram_clear()
    def first(c):
        arrive(0, c)

        @pl.loop(0, per)
        def _(j):
            s = c * per + j
            value = apply_far(s, halo)
            here, low = split(value)
            full[s] = value
            image[s] = here
            rounded[s] = low
            for d in range(4):
                u_out[d, s] = mul(lk[d + 1, s], here, TURNED).astype(bf16)

        gram_add(image[sites(c)], rounded[sites(c)])

    for c in range(CHUNKS):
        first(c)
        if c < EARLY[1]:
            send(1, c)
        if c == EARLY[0] - 1:
            sum_gather(0)
        if c == EARLY[0]:
            sums[0] = sum_done(0)
            elimination_begin(sums[0], work)
        if EARLY[0] <= c < CHUNKS - 1:
            eliminate(work.at[0], *share(c - EARLY[0], CHUNKS - EARLY[0]))

    sum_start(1, gram_ref[...] + 0.5 * (cross_ref[...] + cross_ref[...].T))
    adjoint_near(0, per * 2)
    sum_spread(1)
    send_range(1, EARLY[1], CHUNKS)
    adjoint_near(per * 2, n)
    gram_clear()
    eliminate(work.at[0], share(CHUNKS - 1 - EARLY[0], CHUNKS - EARLY[0])[0], rhs)
    inverse0[...] = elimination_end(sums[0], work)

    def second(c):
        arrive(1, c)

        @pl.loop(0, per)
        def _(j):
            s = c * per + j
            value = acc[s]
            for d in range(4):
                value = value + u_in[d, s].astype(f32)
            normal[s] = value
            rounded[s] = value.astype(bf16)

    def residual(c):
        value, high = normal[sites(c)], rounded[sites(c)]
        return r[sites(c)].astype(f32) - times(high, (value - high.astype(f32)).astype(bf16), 0)

    def third(c):
        gram_add(*split(residual(c)))

    ahead = CHUNKS - 2
    for c in range(ahead):
        second(c)
        if c < EARLY[2]:
            send(2, c)
        if c == 0:
            sum_gather(1)
            sums[1] = sum_done(1)
            elimination_begin(sums[1], work)
        eliminate(work.at[0], *share(c, ahead))
    keep(0, solved(sums[1], elimination_end(sums[1], work), sums[0]))

    @pl.loop(0, ahead)
    def _(c):
        third(c)

    @pl.loop(ahead, CHUNKS)
    def _(c):
        second(c)
        third(c)

    sum_start(2, gram_ref[...] + cross_ref[...] + cross_ref[...].T)
    apply_near(rounded, lambda s: normal[s], 0, per * 2)
    sum_spread(2)
    send_range(2, EARLY[2], CHUNKS)
    apply_near(rounded, lambda s: normal[s], per * 2, n)
    gram_clear()
    @pl.loop(0, CHUNKS)
    def _(c):
        for copy in copies(1, c):
            copy.wait_send()

    def fourth(c):
        for dirs in ((0, 1), (2,), (3,)) if c == CHUNKS - 1 else ((0, 1, 2, 3),):
            for d in dirs:
                vector_copy(2, d, c, rounded, halo).wait_recv()
            for j in range(per):
                s = c * per + j
                total = acc[s]
                for d in dirs:
                    total = total + mul(lk[d + 1, s], halo[d, s], STRAIGHT)
                acc[s] = total

        here = (full[sites(c)] - times(*split(acc[sites(c)]), 0)).astype(bf16)
        gram_ref[...] += gram(here, here)

    def fifth(c):
        high, low = split(residual(c) + source_times(c, 1))
        u_out[0, sites(c)] = high
        u_out[1, sites(c)] = low
        normal[sites(c)] = source_times(c, 0)

    front, back = pl.ds(0, n // 2), pl.ds(n // 2, n // 2)
    outs = [pltpu.make_async_copy(source, target, local_sem.at[2 + k]) for k, (source, target) in enumerate(
        ((normal.at[front], first_ref), (normal.at[back], second_ref), (u_out.at[0], high_ref), (u_out.at[1], low_ref)))]
    begin = EARLY[2] + 1
    for c in range(CHUNKS):
        fourth(c)
        if c == EARLY[2] - 1:
            sum_gather(2)
        if c == EARLY[2]:
            fresh_ref[...] = sum_done(2)
            beta = solved(sums[0], inverse0[...], fresh_ref[...])
            keep(1, beta)
            curvature_ref[...] = dot_t(beta, dot(sums[1], beta))
        if begin <= c < CHUNKS - 1:
            lo, hi = share(c - begin, CHUNKS - 1 - begin, CHUNKS)
            pl.loop(lo, hi)(fifth)
        if c == CHUNKS - 2:
            for copy in outs:
                copy.start()

    sum_start(3, gram_ref[...])
    sum_spread(3)
    sum_gather(3)
    for copy in outs:
        copy.wait()
    for stage in (0, 2):
        @pl.loop(0, CHUNKS)
        def _(c):
            for copy in copies(stage, c):
                copy.wait_send()
    curvature = sum_done(3) - curvature_ref[...]
    curvature_ref[...] = 0.5 * (curvature + curvature.T)
    for k in range(SUMS):
        sum_waits(k)


def krylov(sources, links, sizes):
    ny, nt, nx, nz, comp, rhs = sources.shape
    assert nt == 1 and nx == 1
    n = ny * nz
    n_ta, n_xy = sizes["ta"], sizes["xy"]
    rows = piece_rows(rhs, n_ta)
    anywhere = pl.BlockSpec(memory_space=pl.ANY)
    vmem = pl.BlockSpec(memory_space=pltpu.VMEM)
    slab = lambda *lead: pltpu.VMEM(lead + (n, comp, rhs), bf16)
    wide = pltpu.VMEM((n, comp, rhs), f32)
    pieces = lambda count: pltpu.VMEM((SUMS, count, rows, rhs // 2), f32)
    most = max(n_ta, n_xy)
    square = lambda *lead: pltpu.VMEM(lead + (rhs, rhs), f32)
    return pl.pallas_call(
        functools.partial(krylov_kernel, sizes, ny, nz),
        out_shape=[jax.ShapeDtypeStruct((n // 2, comp, rhs), f32)] * 2 + [jax.ShapeDtypeStruct((n, comp, rhs), bf16)] * 2
        + [jax.ShapeDtypeStruct((rhs, rhs), f32)] * 2,
        in_specs=[anywhere, anywhere],
        out_specs=[anywhere] * 4 + [vmem] * 2,
        scratch_shapes=[
            slab(), pltpu.VMEM((links.shape[0], n, comp, comp), bf16), slab(4), slab(4), slab(4), slab(), slab(),
            wide, wide, wide, square(), square(), square(2), square(), square(2), pltpu.VMEM((4, rhs, rhs), bf16),
            pieces(n_ta), pieces(n_ta), pltpu.VMEM((SUMS, rows, rhs // 2), f32), pieces(n_xy), pieces(n_ta),
            pltpu.SemaphoreType.DMA((6,)), pltpu.SemaphoreType.DMA((3, 4, CHUNKS)), pltpu.SemaphoreType.DMA((3, 4, CHUNKS)),
            pltpu.SemaphoreType.DMA((SUMS, 3, PARTS, most)), pltpu.SemaphoreType.DMA((SUMS, 3, PARTS, most)),
        ],
        cost_estimate=pl.CostEstimate(flops=int(6e9), bytes_accessed=64 << 20, transcendentals=0),
        compiler_params=pltpu.CompilerParams(collective_id=0, has_side_effects=True, vmem_limit_bytes=46 << 20),
    )(sources.reshape(n, comp, rhs), links.reshape(links.shape[0], n, comp, comp))


dot = functools.partial(jnp.dot, precision=HI, preferred_element_type=f32)


def dot_t(a, b):
    return lax.dot_general(a, b, TURNED, precision=HI, preferred_element_type=f32)


def split(value):
    high = value.astype(bf16)
    return high, (value - high.astype(f32)).astype(bf16)


def scaled(a):
    row, col = iotas(a.shape[0])
    eye = jnp.where(row == col, 1.0, 0.0).astype(f32)
    diag = a * eye
    down = lax.rsqrt(jnp.sum(diag, axis=1, keepdims=True))
    across = lax.rsqrt(jnp.sum(diag, axis=0, keepdims=True))
    return a * down * across, eye, down, across


def eliminate(x_ref, lo, hi):
    row, col = iotas(x_ref.shape[0])

    def step(k, carry):
        m = x_ref[...]
        pivot_row = x_ref[pl.ds(k, 1), :]
        here = col == k
        pivot_col = jnp.sum(jnp.where(here, m, 0.0), axis=1, keepdims=True)
        hit = here[:1]
        inv = 1.0 / jnp.sum(jnp.where(hit, pivot_row, 0.0), axis=1, keepdims=True)
        line = jnp.where(hit, inv, pivot_row * inv)
        m = jnp.where(here, 0.0, m) - pivot_col * line
        x_ref[...] = jnp.where(row == k, line, m)
        return carry

    lax.fori_loop(lo, hi, step, 0)


def elimination_begin(a, work):
    work[0] = work[1] = scaled(a)[0]


def elimination_end(a, work):
    _, eye, down, across = scaled(a)
    return refined(work[1], work[0], eye, down, across)


def refined(a, x, eye, down, across):
    x = x + dot(x, eye - dot(a, x))
    return x * down * across


def solved(a, inverse, right):
    out = dot(inverse, right)
    return out + dot(inverse, right - dot(a, out))


def solve(a, right, x_ref, s_ref, out_ref):
    s, eye, down, across = scaled(a)
    power = eye - s
    near = power.astype(bf16)
    square = mul(near, near, STRAIGHT)
    near2 = square.astype(bf16)
    fourth = mul(near2, near2, STRAIGHT).astype(bf16)
    inverse = eye + power + square + mul(near, near2, STRAIGHT)
    inverse = (inverse + mul(inverse.astype(bf16), fourth, STRAIGHT)).astype(bf16)
    off = jnp.abs(eye - mul(s.astype(bf16), inverse, STRAIGHT))
    worst = jnp.max(jnp.sum(off, axis=1, keepdims=True))
    right = right * down
    x = mul(inverse, right.astype(bf16), STRAIGHT)
    for _ in range(2):
        x = x + mul(inverse, (right - dot(s, x)).astype(bf16), STRAIGHT)
    out_ref[...] = x * down

    @pl.when(jnp.logical_not(worst < 0.05))
    def _():
        s_ref[...] = s
        x_ref[...] = s
        eliminate(x_ref, 0, a.shape[0])
        x = refined(s_ref[...], x_ref[...], eye, 1.0, 1.0)
        out_ref[...] = solved(s_ref[...], x, right) * down


def closing_kernel(chunks, curvature_ref, fresh_ref, first, second, high, low, out_hbm, out, coef, x_ref, s_ref, alpha_ref, store_sem):
    n, comp, rhs = high.shape
    per = n // chunks
    solve(curvature_ref[...], fresh_ref[...], x_ref, s_ref, alpha_ref)
    coef[0], coef[1] = split(alpha_ref[...])

    def store(c):
        return pltpu.make_async_copy(out.at[pl.ds(c * per, per)], out_hbm.at[pl.ds(c * per, per)], store_sem.at[c])

    for base, lo in ((first, 0), (second, chunks // 2)):
        @pl.loop(0, chunks // 2)
        def _(c):
            here = pl.ds((lo + c) * per, per)
            left, rest = high[here].reshape(-1, rhs), low[here].reshape(-1, rhs)
            step = mul(left, coef[0], STRAIGHT) + mul(left, coef[1], STRAIGHT) + mul(rest, coef[0], STRAIGHT)
            out[here] = base[pl.ds(c * per, per)] + step.reshape(per, comp, rhs)
            store(lo + c).start()

    @pl.loop(0, chunks)
    def _(c):
        store(c).wait()


def closing(first, second, high, low, curvature, fresh):
    vmem, anywhere = pl.BlockSpec(memory_space=pltpu.VMEM), pl.BlockSpec(memory_space=pl.ANY)
    rhs = fresh.shape[0]
    return pl.pallas_call(
        functools.partial(closing_kernel, CHUNKS // 2),
        out_shape=jax.ShapeDtypeStruct(high.shape, f32),
        in_specs=[vmem] * 6,
        out_specs=anywhere,
        scratch_shapes=[pltpu.VMEM(high.shape, f32), pltpu.VMEM((2, rhs, rhs), bf16)] + [pltpu.VMEM((rhs, rhs), f32)] * 3
        + [pltpu.SemaphoreType.DMA((CHUNKS,))],
        cost_estimate=pl.CostEstimate(flops=int(4e9), bytes_accessed=10 << 20, transcendentals=0),
        compiler_params=pltpu.CompilerParams(vmem_limit_bytes=20 << 20),
    )(curvature, fresh, first, second, high, low)


def solution(mesh):
    sizes = {axis: mesh.shape[axis] for axis in ("ta", "xy")}

    def body(sources, links):
        return closing(*krylov(sources, links, sizes)).reshape(sources.shape)

    return jax.shard_map(
        body,
        mesh=mesh,
        in_specs=(
            P("groups", "ta", "xy", None, None, None),
            P("groups", None, "ta", "xy", None, None, None),
        ),
        out_specs=P("groups", "ta", "xy", None, None, None),
        check_vma=False,
    )
```
